256 devices in a mesh: section: 2 (over y_hi), seq: 32 (over x, z), chan: 4 (over y_lo, core).
Axes of the slice: x: 4, y: 4 (y_hi: 2, y_lo: 2; y = y_hi * 2 + y_lo), z: 8, core: 2. Of those that a mesh axis runs over, the one named last changes fastest.
Arguments:
- bases: int32 [2, 2097152], P('section', 'seq'), may hold values from 0 to 3
- stem_embedding_weight: bfloat16 [512, 1536], P(None, 'chan'), may hold values from -1.64443437 to 1.64443437
- gains: float32 [3, 1536], replicated, may hold values from 0.1 to 1.9
- conv_weight: bfloat16 [3, 3, 1536, 1536], P(None, None, None, 'chan'), may hold values from -0.09375 to 0.09375
- dec_weight: bfloat16 [1536, 384], P('chan'), may hold values from -0.3125 to 0.3125
- upstream: bfloat16 [2, 16384, 1536], P('section', 'seq', 'chan'), may hold values from -0.032958984 to 0.032958984
Outputs:
- decoded: bfloat16 [2, 16384, 1536], P('section', 'seq', 'chan')
- weight_grad: float32 [1536, 384], P('chan')
The draws below stay inside these ranges and needn't reach their ends.
All inputs are finite; a program needn't handle non-finite values.
Results may differ from the reference program's by a relative error of at most 0.0076.
Values may be sent and summed in bfloat16 or wider, within the bound.
No kernel may reach another device: no remote copies, remote signals or barrier semaphores. Data moves between devices by JAX's collectives and lax.ppermute only.
A program may use at most 128 MiB of HBM per device.

```python
import math
import jax
import jax.numpy as jnp
from jax import lax

D = 1536
G = 4
DG = 384
PATCH = 128
KERNEL = 3
FIRST_DILATION0 = 2
LAYERS = 3
BINS = 16384
BASES = 2097152
SEQS = 2


def draw_stem_embedding_weight(key, part):
    key_normal = jax.random.fold_in(key, 11)
    key_rows = jax.random.fold_in(key, 12)
    key_cols = jax.random.fold_in(key, 13)
    values = jnp.clip(jax.random.normal(key_normal, (PATCH * 4, D), jnp.float32), -4.0, 4.0)
    row_scale = jnp.exp(jax.random.uniform(key_rows, (PATCH * 4, 1), jnp.float32) * math.log(10.0))
    col_scale = jnp.exp(jax.random.uniform(key_cols, (1, D), jnp.float32) * math.log(10.0))
    norm_factor = 21.5
    result = values * row_scale * col_scale / (norm_factor * math.sqrt(PATCH))
    return result.astype(jnp.bfloat16)


def plant(array, key, least, high):
    index_at = [jax.random.randint(jax.random.fold_in(key, axis), (), 0, length) for axis, length in enumerate(array.shape)]
    longest = array.shape.index(max(array.shape))
    beside = index_at[:longest] + [(index_at[longest] + 1) % array.shape[longest]] + index_at[longest + 1:]
    return array.at[tuple(index_at)].set(least).at[tuple(beside)].set(high)


def block_scale(own_key, extent, split, least, largest):
    loudness = 1.0
    for dim, blocks in split:
        steps = jax.random.uniform(jax.random.fold_in(jax.random.fold_in(own_key, 6), dim), (blocks,), jnp.float32, least / len(split), largest / len(split))
        loudness = loudness * jnp.repeat(jnp.exp(steps), extent[dim] // blocks).reshape((-1,) + (1,) * (len(extent) - 1 - dim))
    return loudness


def centred(stream_key, shape, width, limit, split=(), held_as=jnp.bfloat16):
    level = block_scale(stream_key, shape, split, -0.22, 0.18) if split else 1.0
    values = jax.random.normal(stream_key, shape, jnp.float32) * width * level
    return jnp.minimum(jnp.maximum(values, -limit), limit).astype(held_as)


def setup_inputs(seed: int = 0) -> dict:
    arg_keys = jax.random.split(jax.random.key(seed), 7)
    bases = plant(jax.random.randint(arg_keys[0], (SEQS, BASES), 0, 4), jax.random.fold_in(arg_keys[0], 1), 0, 3).astype(jnp.int32)
    stem_embedding_weight = draw_stem_embedding_weight(jax.random.fold_in(arg_keys[6], 71), 0)
    gains = jnp.clip(1.0 + 0.18 * jax.random.normal(arg_keys[2], (LAYERS, D), jnp.float32), 0.1, 1.9)
    conv_weight = centred(arg_keys[3], (LAYERS, KERNEL, D, D), (KERNEL * D) ** -0.5, 0.09375, ((3, 4),))
    dec_weight = centred(arg_keys[4], (D, DG), DG ** -0.5, 0.3125, ((0, 4),))
    upstream = centred(arg_keys[5], (SEQS, BINS, D), ((SEQS * BINS) ** -0.5), 0.032958984, ((0, 2), (1, 32), (2, 4)))
    return {"bases": bases, "stem_embedding_weight": stem_embedding_weight, "gains": gains, "conv_weight": conv_weight, "dec_weight": dec_weight, "upstream": upstream}


EPSILON = 1e-06

def activate(rows, gain_row):
    widened = rows.astype(jnp.float32)
    inverse_rms = lax.rsqrt(lax.optimization_barrier(jnp.mean(widened * widened, axis=-1, keepdims=True)) + EPSILON)
    return jax.nn.gelu(widened * inverse_rms * gain_row).astype(jnp.bfloat16)

def reference(bases, stem_embedding_weight, gains, conv_weight, dec_weight, upstream):
    letters = bases.reshape(SEQS, BINS, PATCH)
    group_weights = dec_weight.astype(jnp.float32).reshape(G, DG, DG)
    total_grad = jnp.zeros((G, DG, DG), jnp.float32)
    decoded_list = []
    for seq_index in range(SEQS):
        onehot = letters[seq_index][:, :, None] == jnp.arange(4, dtype=jnp.int32)[None, None, :]
        onehot = onehot.astype(jnp.bfloat16).reshape(BINS, PATCH * 4)
        stream = jnp.dot(onehot, stem_embedding_weight, preferred_element_type=jnp.float32).astype(jnp.bfloat16)
        for tower_layer_index in range(LAYERS):
            dilation_step = FIRST_DILATION0 * 2 ** tower_layer_index
            normed = activate(stream, gains[tower_layer_index])
            padded = jnp.pad(normed, ((dilation_step, dilation_step), (0, 0)))
            update = jnp.zeros((BINS, D), jnp.float32)
            for offset in range(KERNEL):
                start = offset * dilation_step
                update = update + jnp.dot(padded[start:start + BINS], conv_weight[tower_layer_index, offset], preferred_element_type=jnp.float32)
            stream = (stream.astype(jnp.float32) + update).astype(jnp.bfloat16)
        grouped_decoder = stream.astype(jnp.float32).reshape(BINS, G, DG)
        decoded = jnp.einsum('bgi,gij->bgj', grouped_decoder, group_weights).reshape(BINS, D).astype(jnp.bfloat16)
        decoded_list.append(decoded)
        upstream_rows = upstream[seq_index].astype(jnp.float32).reshape(BINS, G, DG)
        total_grad = total_grad + jnp.einsum('bgi,bgj->gij', grouped_decoder, upstream_rows)
    return (jnp.stack(decoded_list), total_grad.reshape(D, DG))
```

```python
import functools

import jax
import jax.numpy as jnp
from jax import lax
from jax.experimental import pallas as pl
from jax.experimental.pallas import tpu as pltpu
from jax.sharding import PartitionSpec as P

PATCH = 128
FIRST_DILATION0 = 2
EPSILON = 1e-06
HALO = 16
PAD = 16

VMEM = pl.BlockSpec(memory_space=pltpu.VMEM)
SMEM = pl.BlockSpec(memory_space=pltpu.SMEM)
ANY = pl.BlockSpec(memory_space=pl.ANY)


def gelu(x):
    inner = x * (0.7978845608028654 + 0.035677408136300125 * (x * x))
    return (0.5 * x) * (1.0 + jnp.tanh(inner))


def norm_rows(ids, layer, pieces, gains_ref, normed, first, rows, width):
    wide = [p.astype(jnp.float32) for p in pieces]
    total = wide[0] * wide[0]
    for w in wide[1:]:
        total = total + w * w
    inverse = lax.rsqrt(jnp.sum(total, axis=-1, keepdims=True) * (1.0 / (4 * width)) + EPSILON)
    for k, w in enumerate(wide):
        value = gelu(w * inverse * gains_ref[layer, ids[0] ^ k])
        normed[pl.ds(PAD + first, rows), k * width : (k + 1) * width] = value.astype(jnp.bfloat16)


def in_sequence(ids, rows, bins, count):
    bin_at = lax.broadcasted_iota(jnp.int32, (rows, 1), 0) + (ids[1] * bins - HALO)
    return jnp.where((bin_at >= 0) & (bin_at < count), 1.0, 0.0)


def start_weights(ids, layer, w_hbm, w_vmem, sems, width):
    copies = []
    for t in range(3):
        for k in range(4):
            group = ids[0] ^ k
            copies.append(
                pltpu.make_async_copy(
                    w_hbm.at[layer, t, pl.ds(group * width, width), :],
                    w_vmem.at[t, pl.ds(k * width, width), :],
                    sems.at[t, k],
                )
            )
            copies[-1].start()
    return copies


def convolve(normed, w_vmem, first, rows, dilation):
    update = None
    for t in range(3):
        part = jnp.dot(
            normed[pl.ds(PAD + first + (t - 1) * dilation, rows), :],
            w_vmem[t],
            preferred_element_type=jnp.float32,
        )
        update = part if update is None else update + part
    return update


def clear_pads(normed, rows):
    zeros = jnp.zeros((PAD, normed.shape[1]), normed.dtype)
    normed[0:PAD, :] = zeros
    normed[PAD + rows : PAD + rows + PAD, :] = zeros


def first_layer(bins, count, ids, before, own, after, *refs):
    w_stem, (gains, w_hbm, out, normed, stream, w_vmem, sems) = refs[:6], refs[6:]
    width = out.shape[1]
    rows = bins + 2 * HALO
    copies = start_weights(ids, 0, w_hbm, w_vmem, sems, width)
    clear_pads(normed, rows)
    letters = jnp.concatenate([before[...], own[...], after[...]], axis=0)
    letters = letters.astype(jnp.float32).astype(jnp.bfloat16)
    lane = lax.broadcasted_iota(jnp.int32, (PATCH, 4 * PATCH), 1)
    row = lax.broadcasted_iota(jnp.int32, (PATCH, 4 * PATCH), 0)
    spread = jnp.where(lane // 4 == row, 1.0, 0.0).astype(jnp.bfloat16)
    repeated = jnp.dot(letters, spread, preferred_element_type=jnp.float32)
    base = (lax.broadcasted_iota(jnp.int32, (1, 4 * PATCH), 1) % 4).astype(jnp.float32)
    inside = in_sequence(ids, rows, bins, count)
    onehot = (jnp.where(repeated == base, 1.0, 0.0) * inside).astype(jnp.bfloat16)
    half = 2 * PATCH
    stream[:, 0:width] = jnp.dot(
        onehot, w_stem[0][...], preferred_element_type=jnp.float32
    ).astype(jnp.bfloat16)
    stream[:, width : 2 * width] = jnp.dot(
        onehot, w_stem[1][...], preferred_element_type=jnp.float32
    ).astype(jnp.bfloat16)
    for k in (2, 3):
        low, high = w_stem[2 * k - 2], w_stem[2 * k - 1]
        value = jnp.dot(onehot[:, :half], low[...], preferred_element_type=jnp.float32)
        value = value + jnp.dot(onehot[:, half:], high[...], preferred_element_type=jnp.float32)
        stream[:, k * width : (k + 1) * width] = value.astype(jnp.bfloat16)

    step = 32

    @pl.loop(0, rows // step)
    def _(i):
        first = pl.multiple_of(i * step, step)
        pieces = [stream[pl.ds(first, step), k * width : (k + 1) * width] for k in range(4)]
        norm_rows(ids, 0, pieces, gains, normed, first, step, width)

    for copy in copies:
        copy.wait()
    update = convolve(normed, w_vmem, 0, rows, FIRST_DILATION0)
    total = (stream[:, 0:width].astype(jnp.float32) + update) * inside
    out[...] = total.astype(jnp.bfloat16)


def middle_layer(bins, count, ids, s0, s1, s2, s3, gains, w_hbm, out, normed, w_vmem, sems):
    width = out.shape[1]
    rows = bins + 2 * HALO
    copies = start_weights(ids, 1, w_hbm, w_vmem, sems, width)
    clear_pads(normed, rows)
    step = 32

    @pl.loop(0, rows // step)
    def _(i):
        first = pl.multiple_of(i * step, step)
        pieces = [s[pl.ds(first, step), :] for s in (s0, s1, s2, s3)]
        norm_rows(ids, 1, pieces, gains, normed, first, step, width)

    for copy in copies:
        copy.wait()
    update = convolve(normed, w_vmem, 0, rows, 2 * FIRST_DILATION0)
    total = (s0[...].astype(jnp.float32) + update) * in_sequence(ids, rows, bins, count)
    out[...] = total.astype(jnp.bfloat16)


def last_layer(
    bins, ids, s0, s1, s2, s3, gains, w_hbm, upstream,
    out, g0, g1, g2, g3, normed, w_vmem, grad, sems,
):
    width = out.shape[1]
    rows = bins + 2 * HALO
    copies = start_weights(ids, 2, w_hbm, w_vmem, sems, width)
    step = 32

    @pl.loop(0, rows // step)
    def _(i):
        first = pl.multiple_of(i * step, step)
        pieces = [s[pl.ds(first, step), :] for s in (s0, s1, s2, s3)]
        norm_rows(ids, 2, pieces, gains, normed, first, step, width)

    for copy in copies:
        copy.wait()
    update = convolve(normed, w_vmem, HALO, bins, 4 * FIRST_DILATION0)
    total = (s0[HALO : HALO + bins, :].astype(jnp.float32) + update).astype(jnp.bfloat16)
    out[...] = total
    grad[...] = lax.dot_general(
        total, upstream[...], (((0,), (0,)), ((), ())), preferred_element_type=jnp.float32
    )
    quarter = width // 4
    g0[...] = grad[pl.ds(pl.multiple_of(ids[2] * quarter, 8), quarter), :]
    for k, g in ((1, g1), (2, g2), (3, g3)):
        at = pl.multiple_of((ids[2] ^ k) * quarter, 8)
        g[...] = grad[pl.ds(at, quarter), :].astype(jnp.bfloat16)


def assemble(ids, p0, p1, p2, p3, out):
    quarter = p0.shape[0]
    for k, p in enumerate((p0, p1, p2, p3)):
        at = pl.multiple_of((ids[2] ^ k) * quarter, 8)
        out[pl.ds(at, quarter), :] = p[...].astype(jnp.float32)


def pairs(size, partner):
    return [(i, partner(i)) for i in range(size)]


def body(zs, seq_count, bases, stem, gains, conv_weight, dec_weight, upstream):
    bins, width = upstream.shape[1], upstream.shape[2]
    rows = bins + 2 * HALO
    count = bins * seq_count
    seq, chan = lax.axis_index("seq"), lax.axis_index("chan")
    x, z = seq // zs, seq % zs
    x_half, z_half = ((x + 1) // 2) % 2, ((z + 1) // 2) % 2
    ids = jnp.stack([chan, seq, x_half * 2 + z_half]).astype(jnp.int32)

    across = functools.partial(lax.ppermute, axis_name="chan", perm=pairs(4, lambda i: i ^ 2))
    other_core = functools.partial(lax.ppermute, axis_name="chan", perm=pairs(4, lambda i: i ^ 1))
    far = functools.partial(
        lax.ppermute, axis_name=("section", "chan"), perm=pairs(8, lambda i: i ^ 6)
    )

    letters = bases.reshape(bins, PATCH)
    up = [(i, i + 1) for i in range(seq_count - 1)]
    down = [(j, i) for i, j in up]
    half = stem.shape[0] // 2
    w2a = across(stem[:half])
    w2b = far(stem[half:])
    w1 = other_core(stem)
    before = lax.ppermute(letters[bins - HALO :], "seq", up)
    after = lax.ppermute(letters[:HALO], "seq", down)
    w3a = other_core(w2a)
    w3b = other_core(w2b)

    gain_rows = gains.reshape(gains.shape[0], 4, 1, width)

    scratch = [
        pltpu.VMEM((rows + 2 * PAD, 4 * width), jnp.bfloat16),
    ]
    weights = [
        pltpu.VMEM((3, 4 * width, width), jnp.bfloat16),
        pltpu.SemaphoreType.DMA((3, 4)),
    ]
    params = pltpu.CompilerParams(vmem_limit_bytes=40 * 2**20)
    stream_shape = jax.ShapeDtypeStruct((rows, width), jnp.bfloat16)
    stream = pl.pallas_call(
        functools.partial(first_layer, bins, count),
        out_shape=stream_shape,
        in_specs=[SMEM] + [VMEM] * 10 + [ANY],
        out_specs=VMEM,
        scratch_shapes=scratch + [pltpu.VMEM((rows, 4 * width), jnp.bfloat16)] + weights,
        compiler_params=params,
        name="layer_zero",
    )(ids, before, letters, after, stem, w1, w2a, w2b, w3a, w3b, gain_rows, conv_weight)

    def gathered(own):
        remote = across(own)
        return own, other_core(own), remote, other_core(remote)

    stream = pl.pallas_call(
        functools.partial(middle_layer, bins, count),
        out_shape=stream_shape,
        in_specs=[SMEM] + [VMEM] * 5 + [ANY],
        out_specs=VMEM,
        scratch_shapes=scratch + weights,
        compiler_params=params,
        name="layer_one",
    )(ids, *gathered(stream), gain_rows, conv_weight)

    quarter = jax.ShapeDtypeStruct((width // 4, width), jnp.bfloat16)
    stream, g0, g1, g2, g3 = pl.pallas_call(
        functools.partial(last_layer, bins),
        out_shape=(
            jax.ShapeDtypeStruct((bins, width), jnp.bfloat16),
            jax.ShapeDtypeStruct((width // 4, width), jnp.float32),
            quarter,
            quarter,
            quarter,
        ),
        in_specs=[SMEM] + [VMEM] * 5 + [ANY, VMEM],
        out_specs=(VMEM,) * 5,
        scratch_shapes=scratch + weights[:1] + [pltpu.VMEM((width, width), jnp.float32)] + weights[1:],
        compiler_params=params,
        name="layer_two",
    )(ids, *gathered(stream), gain_rows, conv_weight, upstream[0])
    decoded = jnp.dot(stream, dec_weight, preferred_element_type=jnp.float32).astype(jnp.bfloat16)

    def over(fx, fz):
        def partner(i):
            return fx(i // zs) * zs + fz(i % zs)

        return functools.partial(lax.ppermute, axis_name="seq", perm=pairs(seq_count, partner))

    def same(i):
        return i

    def flip(i):
        return i ^ 1

    def xs_near(i):
        return 3 - i

    def zs_near(i):
        return (i + 1) % zs if i % 2 else (i - 1) % zs

    def zs_far(i):
        return {0: 3, 3: 0, 1: 6, 6: 1, 2: 5, 5: 2, 4: 7, 7: 4}[i]

    r2 = over(flip, same)(g2)
    r1 = over(same, flip)(g1)
    r3 = over(flip, flip)(g3)
    f32 = jnp.float32
    total = (g0 + r2.astype(f32)) + (r1.astype(f32) + r3.astype(f32))
    own = total.astype(jnp.bfloat16)
    rx = over(xs_near, same)(own)
    rz = over(same, zs_near)(own)
    rxz = over(xs_near, zs_near)(own)
    total = (own.astype(f32) + rx.astype(f32)) + (rz.astype(f32) + rxz.astype(f32))
    own = total.astype(jnp.bfloat16)
    other = lax.ppermute(own, "section", [(0, 1), (1, 0)])
    own = (own.astype(f32) + other.astype(f32)).astype(jnp.bfloat16)
    other = over(same, zs_far)(own)
    own = (own.astype(f32) + other.astype(f32)).astype(jnp.bfloat16)
    r2 = over(flip, same)(own)
    r1 = over(same, flip)(own)
    r3 = over(flip, flip)(own)
    weight_grad = pl.pallas_call(
        assemble,
        out_shape=jax.ShapeDtypeStruct((width, width), jnp.float32),
        in_specs=[SMEM] + [VMEM] * 4,
        out_specs=VMEM,
        name="assemble",
    )(ids, own, r1, r2, r3)
    return (decoded[None], weight_grad)


def solution(mesh):
    placed = (
        P("section", "seq"),
        P(None, "chan"),
        P(),
        P(None, None, None, "chan"),
        P("chan", None),
        P("section", "seq", "chan"),
    )
    seq_count = mesh.shape["seq"]
    return jax.shard_map(
        functools.partial(body, seq_count // 4, seq_count),
        mesh=mesh,
        in_specs=placed,
        out_specs=(P("section", "seq", "chan"), P("chan", None)),
        check_vma=False,
    )
```

```python
import functools

import jax
import jax.numpy as jnp
from jax import lax
from jax.experimental import pallas as pl
from jax.experimental.pallas import tpu as pltpu
from jax.sharding import PartitionSpec as P

PATCH = 128
FIRST_DILATION0 = 2
EPSILON = 1e-06
HALO = 16
STEP = 32
PAD = 16

VMEM = pl.BlockSpec(memory_space=pltpu.VMEM)
SMEM = pl.BlockSpec(memory_space=pltpu.SMEM)
HBM = pl.BlockSpec(memory_space=pltpu.HBM)


def gelu(x):
    inner = x * (0.7978845608028654 + 0.035677408136300125 * (x * x))
    return (0.5 * x) * (1.0 + jnp.tanh(inner))


def in_sequence(ids, first, rows, bins, count):
    bin_at = lax.broadcasted_iota(jnp.int32, (rows, 1), 0) + (ids[1] * bins - HALO + first)
    return jnp.where((bin_at >= 0) & (bin_at < count), 1.0, 0.0)


def norm_rows(ids, layer, pieces, gains, normed, at):
    rows, width = pieces[0].shape
    wide = [p.astype(jnp.float32) for p in pieces]
    total = wide[0] * wide[0]
    for w in wide[1:]:
        total = total + w * w
    inverse = lax.rsqrt(jnp.sum(total, axis=-1, keepdims=True) * (1.0 / (4 * width)) + EPSILON)
    for k, w in enumerate(wide):
        at_lane = pl.multiple_of((ids[0] ^ k) * width, 128)
        value = gelu(w * inverse * gains[layer : layer + 1, pl.ds(at_lane, width)])
        normed[at : at + rows, k * width : (k + 1) * width] = value.astype(jnp.bfloat16)


def norm_segment(ids, layer, read, count, gains, normed, at):
    for first in range(0, count, STEP):
        rows = min(STEP, count - first)
        norm_rows(ids, layer, read(first, rows), gains, normed, at + first)


def convolve(normed, weights, copies, at, rows, dilation):
    update = None
    for t in range(3):
        for copy in copies[t] if copies else ():
            copy.wait()
        first = at + (t - 1) * dilation
        part = jnp.dot(
            normed[first : first + rows, :], weights[t], preferred_element_type=jnp.float32
        )
        update = part if update is None else update + part
    return update


def clear(ref, first, rows):
    ref[first : first + rows, :] = jnp.zeros((rows, ref.shape[1]), ref.dtype)


def start_weights(ids, layer, w_hbm, out, sems):
    width = out.shape[2]
    taps = []
    for t in range(3):
        taps.append([])
        for k in range(4):
            copy = pltpu.make_async_copy(
                w_hbm.at[layer, t, pl.ds((ids[0] ^ k) * width, width), :],
                out.at[t, pl.ds(k * width, width), :],
                sems.at[t, k],
            )
            copy.start()
            taps[-1].append(copy)
    return taps


def one_hot(bins, count, ids, before, own, after, stem_hbm, onehot, stem, sem):
    copy = pltpu.make_async_copy(stem_hbm, stem, sem)
    copy.start()
    letters = jnp.concatenate([before[...], own[...], after[...]], axis=0)
    letters = letters.astype(jnp.float32).astype(jnp.bfloat16)
    lane = lax.broadcasted_iota(jnp.int32, (PATCH, 4 * PATCH), 1)
    row = lax.broadcasted_iota(jnp.int32, (PATCH, 4 * PATCH), 0)
    spread = jnp.where(lane // 4 == row, 1.0, 0.0).astype(jnp.bfloat16)
    repeated = jnp.dot(letters, spread, preferred_element_type=jnp.float32)
    base = (lax.broadcasted_iota(jnp.int32, (1, 4 * PATCH), 1) % 4).astype(jnp.float32)
    inside = in_sequence(ids, 0, bins + 2 * HALO, bins, count)
    onehot[...] = (jnp.where(repeated == base, 1.0, 0.0) * inside).astype(jnp.bfloat16)
    copy.wait()


def first_layer(span, bins, count, ids, onehot, own, w1, w2a, w2b, w3a, w3b, gains, w_in, out, *refs):
    low, high = span
    if low == 0:
        weights, normed, stream, sems = refs
        copies = start_weights(ids, 0, w_in, weights, sems)
    else:
        weights, copies, (normed, stream) = w_in, None, refs
    width = out.shape[1]
    first, last = max(low - HALO, 0), min(high + HALO, bins + 2 * HALO)
    rows = last - first
    clear(normed, 0, PAD)
    clear(normed, PAD + rows, PAD)
    stem = jnp.concatenate(
        [
            own[...],
            w1[...],
            jnp.concatenate([w2a[...], w2b[...]], axis=0),
            jnp.concatenate([w3a[...], w3b[...]], axis=0),
        ],
        axis=1,
    )
    stream[...] = jnp.dot(
        onehot[first:last, :], stem, preferred_element_type=jnp.float32
    ).astype(jnp.bfloat16)

    def read(at, n):
        return [stream[at : at + n, k * width : (k + 1) * width] for k in range(4)]

    norm_segment(ids, 0, read, rows, gains, normed, PAD)
    update = convolve(normed, weights, copies, PAD + low - first, high - low, FIRST_DILATION0)
    total = stream[low - first : high - first, 0:width].astype(jnp.float32) + update
    inside = in_sequence(ids, low, high - low, bins, count)
    out[...] = (total * inside).astype(jnp.bfloat16)


def front(layer, dilation, span, bins, count, ids, *refs):
    pieces, (gains, w_hbm, out, weights, normed, sems) = refs[:4], refs[4:]
    low, high = span
    rows = high + HALO
    copies = start_weights(ids, layer, w_hbm, weights, sems)
    clear(normed, 0, PAD)

    def read(at, n):
        return [p[at : at + n, :] for p in pieces]

    norm_segment(ids, layer, read, rows, gains, normed, PAD)
    update = convolve(normed, weights, copies, PAD + low, high - low, dilation)
    total = pieces[0][low:high, :].astype(jnp.float32) + update
    if count:
        total = total * in_sequence(ids, low, high - low, bins, count)
    out[...] = total.astype(jnp.bfloat16)


def back(layer, dilation, span, bins, count, ids, *refs):
    fronts, backs, (gains, weights, out, normed) = refs[:4], refs[4:8], refs[8:]
    low, high = span
    first = low - HALO
    joint = fronts[0].shape[0]
    rows = joint + backs[0].shape[0] - first
    clear(normed, PAD + rows, PAD)

    def read_front(at, n):
        return [p[first + at : first + at + n, :] for p in fronts]

    def read_back(at, n):
        return [p[at : at + n, :] for p in backs]

    norm_segment(ids, layer, read_front, joint - first, gains, normed, PAD)
    norm_segment(ids, layer, read_back, backs[0].shape[0], gains, normed, PAD + joint - first)
    update = convolve(normed, weights, None, PAD + HALO, high - low, dilation)
    own = jnp.concatenate([fronts[0][low:joint, :], backs[0][0 : high - joint, :]], axis=0)
    total = own.astype(jnp.float32) + update
    if count:
        total = total * in_sequence(ids, low, high - low, bins, count)
    out[...] = total.astype(jnp.bfloat16)


def gradient(stream, upstream):
    return lax.dot_general(
        stream, upstream, (((0,), (0,)), ((), ())), preferred_element_type=jnp.float32
    )


def last_front(span, bins, ids, *refs):
    refs, (upstream, out, grad, weights, normed, sems) = refs[:6], refs[6:]
    front(2, 4 * FIRST_DILATION0, span, bins, 0, ids, *refs, out, weights, normed, sems)
    low, high = span
    grad[...] = gradient(out[...], upstream[low - HALO : high - HALO, :])


def last_back(span, bins, ids, *refs):
    refs, (upstream, before, out, g0, g1, g2, g3, normed, grad) = refs[:10], refs[10:]
    back(2, 4 * FIRST_DILATION0, span, bins, 0, ids, *refs, out, normed)
    low, high = span
    grad[...] = before[...] + gradient(out[...], upstream[low - HALO : high - HALO, :])
    quarter = g0.shape[0]
    g0[...] = grad[pl.ds(pl.multiple_of(ids[2] * quarter, 8), quarter), :]
    for k, g in ((1, g1), (2, g2), (3, g3)):
        at = pl.multiple_of((ids[2] ^ k) * quarter, 8)
        g[...] = grad[pl.ds(at, quarter), :].astype(jnp.bfloat16)


def decode(front_rows, back_rows, weights, out):
    cut = front_rows.shape[0]
    for part, first in ((front_rows, 0), (back_rows, cut)):
        value = jnp.dot(part[...], weights[...], preferred_element_type=jnp.float32)
        out[first : first + part.shape[0], :] = value.astype(jnp.bfloat16)


def assemble(ids, p0, p1, p2, p3, out):
    quarter = p0.shape[0]
    for k, p in enumerate((p0, p1, p2, p3)):
        at = pl.multiple_of((ids[2] ^ k) * quarter, 8)
        out[pl.ds(at, quarter), :] = p[...].astype(jnp.float32)


def tie(value, *done):
    return lax.optimization_barrier((value, *done))[0]


def pairs(size, partner):
    return [(i, partner(i)) for i in range(size)]


def call(name, kernel, outs, in_specs, scratch=(), flops=0, megabytes=52):
    many = isinstance(outs, (list, tuple))
    return pl.pallas_call(
        kernel,
        out_shape=tuple(outs) if many else outs,
        in_specs=in_specs,
        out_specs=(VMEM,) * len(outs) if many else VMEM,
        scratch_shapes=list(scratch),
        compiler_params=pltpu.CompilerParams(vmem_limit_bytes=megabytes * 2**20),
        cost_estimate=pl.CostEstimate(flops=flops, bytes_accessed=2**20, transcendentals=0),
        name=name,
    )


def body(zs, seq_count, bases, stem, gains, conv_weight, dec_weight, upstream):
    bins, width = upstream.shape[1], upstream.shape[2]
    rows = bins + 2 * HALO
    count = bins * seq_count
    bf16, f32 = jnp.bfloat16, jnp.float32
    seq, chan = lax.axis_index("seq"), lax.axis_index("chan")
    x, z = seq // zs, seq % zs
    x_half, z_half = ((x + 1) // 2) % 2, ((z + 1) // 2) % 2
    ids = jnp.stack([chan, seq, x_half * 2 + z_half]).astype(jnp.int32)

    across = functools.partial(lax.ppermute, axis_name="chan", perm=pairs(4, lambda i: i ^ 2))
    other_core = functools.partial(lax.ppermute, axis_name="chan", perm=pairs(4, lambda i: i ^ 1))
    far = functools.partial(
        lax.ppermute, axis_name=("section", "chan"), perm=pairs(8, lambda i: i ^ 6)
    )

    letters = bases.reshape(bins, PATCH)
    up = [(i, i + 1) for i in range(seq_count - 1)]
    down = [(j, i) for i, j in up]
    half = stem.shape[0] // 2
    before = lax.ppermute(letters[bins - HALO :], "seq", up)
    after = lax.ppermute(letters[:HALO], "seq", down)
    w2a = across(stem[:half])
    w2b = far(stem[half:])
    w1 = other_core(stem)
    onehot, stem = call(
        "one_hot",
        functools.partial(one_hot, bins, count),
        [jax.ShapeDtypeStruct((rows, 4 * PATCH), bf16), jax.ShapeDtypeStruct(stem.shape, bf16)],
        [SMEM] + [VMEM] * 3 + [HBM],
        [pltpu.SemaphoreType.DMA],
        megabytes=8,
        flops=10**9,
    )(ids, before, letters, after, stem)
    w2a = tie(w2a, before, after)
    w3a = other_core(w2a)
    w2b = tie(w2b, onehot)
    w3b = other_core(w2b)

    def shape(n):
        return jax.ShapeDtypeStruct((n, width), bf16)

    def work(n):
        return 2 * n * 3 * 4 * width * width

    def normed(n):
        return pltpu.VMEM((n + 2 * PAD, 4 * width), bf16)

    def exchange(own):
        return own, other_core(own), across(own)

    def finish(sent, *done):
        own, beside, remote = sent
        remote = tie(remote, *done)
        return own, beside, remote, other_core(remote)

    cut = bins // 2 + 3 * HALO
    layer_weights = jax.ShapeDtypeStruct((3, 4 * width, width), bf16)
    weight_sems = pltpu.SemaphoreType.DMA((3, 4))
    inputs = (onehot, stem, w1, w2a, w2b, w3a, w3b, gains)
    part, weights = call(
        "zero_front",
        functools.partial(first_layer, (0, cut), bins, count),
        [shape(cut), layer_weights],
        [SMEM] + [VMEM] * 8 + [HBM],
        [normed(cut + HALO), pltpu.VMEM((cut + HALO, 4 * width), bf16), weight_sems],
        flops=work(cut),
    )(ids, *inputs, conv_weight)
    sent_front = exchange(part)
    part = call(
        "zero_back",
        functools.partial(first_layer, (cut, rows), bins, count),
        shape(rows - cut),
        [SMEM] + [VMEM] * 9,
        [normed(rows - cut + HALO), pltpu.VMEM((rows - cut + HALO, 4 * width), bf16)],
        flops=work(rows - cut),
    )(ids, *inputs, weights)
    sent_back = exchange(part)
    fronts = finish(sent_front, part)

    cut = cut - HALO
    part, weights = call(
        "one_front",
        functools.partial(front, 1, 2 * FIRST_DILATION0, (0, cut), bins, count),
        [shape(cut), layer_weights],
        [SMEM] + [VMEM] * 5 + [HBM],
        [normed(cut + HALO), weight_sems],
        flops=work(cut),
    )(ids, *fronts, gains, conv_weight)
    sent_front = exchange(part)
    backs = finish(sent_back, part)
    part = call(
        "one_back",
        functools.partial(back, 1, 2 * FIRST_DILATION0, (cut, rows), bins, count),
        shape(rows - cut),
        [SMEM] + [VMEM] * 10,
        [normed(rows - cut + HALO)],
        flops=work(rows - cut),
    )(ids, *fronts, *backs, gains, weights)
    sent_back = exchange(part)
    fronts = finish(sent_front, part)

    cut = cut - HALO
    front_rows, front_grad, weights = call(
        "two_front",
        functools.partial(last_front, (HALO, cut), bins),
        [shape(cut - HALO), jax.ShapeDtypeStruct((width, width), f32), layer_weights],
        [SMEM] + [VMEM] * 5 + [HBM, VMEM],
        [normed(cut + HALO), weight_sems],
        flops=work(cut - HALO),
    )(ids, *fronts, gains, conv_weight, upstream[0])
    backs = finish(sent_back, front_rows)
    back_rows, g0, g1, g2, g3 = call(
        "two_back",
        functools.partial(last_back, (cut, rows - HALO), bins),
        [shape(rows - HALO - cut), jax.ShapeDtypeStruct((width // 4, width), f32)]
        + [shape(width // 4)] * 3,
        [SMEM] + [VMEM] * 12,
        [normed(rows - cut + HALO), pltpu.VMEM((width, width), f32)],
        flops=work(rows - HALO - cut),
    )(ids, *fronts, *backs, gains, weights, upstream[0], front_grad)
    decoded = call(
        "decode",
        decode,
        shape(bins),
        [VMEM] * 3,
        flops=2 * bins * width * width,
        megabytes=8,
    )(front_rows, back_rows, dec_weight)

    def over(fx, fz):
        def partner(i):
            return fx(i // zs) * zs + fz(i % zs)

        return functools.partial(lax.ppermute, axis_name="seq", perm=pairs(seq_count, partner))

    def same(i):
        return i

    def flip(i):
        return i ^ 1

    def xs_near(i):
        return 3 - i

    def zs_near(i):
        return (i + 1) % zs if i % 2 else (i - 1) % zs

    def zs_far(i):
        return {0: 3, 3: 0, 1: 6, 6: 1, 2: 5, 5: 2, 4: 7, 7: 4}[i]

    r2 = over(flip, same)(g2)
    r1 = over(same, flip)(g1)
    r3 = over(flip, flip)(g3)
    total = (g0 + r2.astype(f32)) + (r1.astype(f32) + r3.astype(f32))
    own = total.astype(bf16)
    rx = over(xs_near, same)(own)
    rz = over(same, zs_near)(own)
    rxz = over(xs_near, zs_near)(own)
    total = (own.astype(f32) + rx.astype(f32)) + (rz.astype(f32) + rxz.astype(f32))
    own = total.astype(bf16)
    other = lax.ppermute(own, "section", [(0, 1), (1, 0)])
    own = (own.astype(f32) + other.astype(f32)).astype(bf16)
    other = over(same, zs_far)(own)
    own = (own.astype(f32) + other.astype(f32)).astype(bf16)
    r2 = over(flip, same)(own)
    r1 = over(same, flip)(own)
    r3 = over(flip, flip)(own)
    weight_grad = call(
        "assemble",
        assemble,
        jax.ShapeDtypeStruct((width, width), f32),
        [SMEM] + [VMEM] * 4,
        megabytes=8,
    )(ids, own, r1, r2, r3)
    return (decoded[None], weight_grad)


def solution(mesh):
    placed = (
        P("section", "seq"),
        P(None, "chan"),
        P(),
        P(None, None, None, "chan"),
        P("chan", None),
        P("section", "seq", "chan"),
    )
    seq_count = mesh.shape["seq"]
    return jax.shard_map(
        functools.partial(body, seq_count // 4, seq_count),
        mesh=mesh,
        in_specs=placed,
        out_specs=(P("section", "seq", "chan"), P("chan", None)),
        check_vma=False,
    )
```

```python
import functools

import jax
import jax.numpy as jnp
from jax import lax
from jax.experimental import pallas as pl
from jax.experimental.pallas import tpu as pltpu
from jax.sharding import PartitionSpec as P

PATCH = 128
FIRST_DILATION0 = 2
EPSILON = 1e-06
HALO = 16
STEP = 32
PAD = 16

VMEM = pl.BlockSpec(memory_space=pltpu.VMEM)
SMEM = pl.BlockSpec(memory_space=pltpu.SMEM)
HBM = pl.BlockSpec(memory_space=pltpu.HBM)


def gelu(x):
    inner = x * (0.7978845608028654 + 0.035677408136300125 * (x * x))
    return (0.5 * x) * (1.0 + jnp.tanh(inner))


def in_sequence(ids, first, rows, bins, count):
    bin_at = lax.broadcasted_iota(jnp.int32, (rows, 1), 0) + (ids[1] * bins - HALO + first)
    return jnp.where((bin_at >= 0) & (bin_at < count), 1.0, 0.0)


def norm_rows(ids, layer, pieces, gains, normed, at):
    rows, width = pieces[0].shape
    wide = [p.astype(jnp.float32) for p in pieces]
    total = wide[0] * wide[0]
    for w in wide[1:]:
        total = total + w * w
    inverse = lax.rsqrt(jnp.sum(total, axis=-1, keepdims=True) * (1.0 / (4 * width)) + EPSILON)
    for k, w in enumerate(wide):
        at_lane = pl.multiple_of((ids[0] ^ k) * width, 128)
        value = gelu(w * inverse * gains[layer : layer + 1, pl.ds(at_lane, width)])
        normed[at : at + rows, k * width : (k + 1) * width] = value.astype(jnp.bfloat16)


def norm_segment(ids, layer, read, count, gains, normed, at):
    for first in range(0, count, STEP):
        rows = min(STEP, count - first)
        norm_rows(ids, layer, read(first, rows), gains, normed, at + first)


def convolve(normed, weights, at, rows, dilation):
    update = None
    for t in range(3):
        first = at + (t - 1) * dilation
        part = jnp.dot(
            normed[first : first + rows, :], weights[t], preferred_element_type=jnp.float32
        )
        update = part if update is None else update + part
    return update


def clear(ref, first, rows):
    ref[first : first + rows, :] = jnp.zeros((rows, ref.shape[1]), ref.dtype)


def start_weights(ids, layer, w_hbm, out, sems):
    width = out.shape[2]
    copies = []
    for t in range(3):
        for k in range(4):
            copies.append(
                pltpu.make_async_copy(
                    w_hbm.at[layer, t, pl.ds((ids[0] ^ k) * width, width), :],
                    out.at[t, pl.ds(k * width, width), :],
                    sems.at[t, k],
                )
            )
            copies[-1].start()
    return copies


def wait_all(copies):
    for copy in copies:
        copy.wait()


def one_hot(bins, count, ids, before, own, after, w_hbm, onehot, weights, sems):
    copies = start_weights(ids, 0, w_hbm, weights, sems)
    letters = jnp.concatenate([before[...], own[...], after[...]], axis=0)
    lane = lax.broadcasted_iota(jnp.int32, (PATCH, 4 * PATCH), 1)
    row = lax.broadcasted_iota(jnp.int32, (PATCH, 4 * PATCH), 0)
    spread = jnp.where(lane // 4 == row, 1.0, 0.0).astype(jnp.bfloat16)
    repeated = jnp.dot(letters, spread, preferred_element_type=jnp.float32)
    base = (lax.broadcasted_iota(jnp.int32, (1, 4 * PATCH), 1) % 4).astype(jnp.float32)
    inside = in_sequence(ids, 0, bins + 2 * HALO, bins, count)
    onehot[...] = (jnp.where(repeated == base, 1.0, 0.0) * inside).astype(jnp.bfloat16)
    wait_all(copies)


def first_layer(span, bins, count, ids, onehot, own_a, own_b, w1, w2a, w2b, w3a, w3b, gains, weights, *refs):
    low, high = span
    if low == 0:
        copies, (out, normed, stream) = [], refs
    else:
        w_hbm, out, later, normed, stream, sems = refs
        copies = start_weights(ids, 1, w_hbm, later, sems)
    width = out.shape[1]
    first, last = max(low - HALO, 0), min(high + HALO, bins + 2 * HALO)
    rows = last - first
    clear(normed, 0, PAD)
    clear(normed, PAD + rows, PAD)
    stem = jnp.concatenate(
        [
            jnp.concatenate([own_a[...], own_b[...]], axis=0),
            w1[...],
            jnp.concatenate([w2a[...], w2b[...]], axis=0),
            jnp.concatenate([w3a[...], w3b[...]], axis=0),
        ],
        axis=1,
    )
    stream[...] = jnp.dot(
        onehot[first:last, :], stem, preferred_element_type=jnp.float32
    ).astype(jnp.bfloat16)

    def read(at, n):
        return [stream[at : at + n, k * width : (k + 1) * width] for k in range(4)]

    norm_segment(ids, 0, read, rows, gains, normed, PAD)
    update = convolve(normed, weights, PAD + low - first, high - low, FIRST_DILATION0)
    total = stream[low - first : high - first, 0:width].astype(jnp.float32) + update
    inside = in_sequence(ids, low, high - low, bins, count)
    out[...] = (total * inside).astype(jnp.bfloat16)
    wait_all(copies)


def front(layer, dilation, span, bins, count, ids, *refs):
    pieces, (gains, weights, out, normed) = refs[:4], refs[4:]
    low, high = span
    rows = high + HALO
    clear(normed, 0, PAD)

    def read(at, n):
        return [p[at : at + n, :] for p in pieces]

    norm_segment(ids, layer, read, rows, gains, normed, PAD)
    update = convolve(normed, weights, PAD + low, high - low, dilation)
    total = pieces[0][low:high, :].astype(jnp.float32) + update
    if count:
        total = total * in_sequence(ids, low, high - low, bins, count)
    out[...] = total.astype(jnp.bfloat16)


def back(layer, dilation, span, bins, count, ids, *refs):
    fronts, backs, (gains, weights) = refs[:4], refs[4:8], refs[8:10]
    copies = []
    if len(refs) == 15:
        w_hbm, out, later, normed, sems = refs[10:]
        copies = start_weights(ids, layer + 1, w_hbm, later, sems)
    else:
        out, normed = refs[10:]
    low, high = span
    first = low - HALO
    joint = fronts[0].shape[0]
    rows = joint + backs[0].shape[0] - first
    clear(normed, PAD + rows, PAD)

    def read_front(at, n):
        return [p[first + at : first + at + n, :] for p in fronts]

    def read_back(at, n):
        return [p[at : at + n, :] for p in backs]

    norm_segment(ids, layer, read_front, joint - first, gains, normed, PAD)
    norm_segment(ids, layer, read_back, backs[0].shape[0], gains, normed, PAD + joint - first)
    update = convolve(normed, weights, PAD + HALO, high - low, dilation)
    own = jnp.concatenate([fronts[0][low:joint, :], backs[0][0 : high - joint, :]], axis=0)
    total = own.astype(jnp.float32) + update
    if count:
        total = total * in_sequence(ids, low, high - low, bins, count)
    out[...] = total.astype(jnp.bfloat16)
    wait_all(copies)


def gradient(stream, upstream):
    return lax.dot_general(
        stream, upstream, (((0,), (0,)), ((), ())), preferred_element_type=jnp.float32
    )


def last_front(span, bins, ids, *refs):
    refs, (upstream, out, grad, normed) = refs[:6], refs[6:]
    front(2, 4 * FIRST_DILATION0, span, bins, 0, ids, *refs, out, normed)
    low, high = span
    grad[...] = gradient(out[...], upstream[low - HALO : high - HALO, :])


def last_back(span, bins, ids, *refs):
    refs, (upstream, before, out, g0, g1, g2, g3, normed, grad) = refs[:10], refs[10:]
    back(2, 4 * FIRST_DILATION0, span, bins, 0, ids, *refs, out, normed)
    low, high = span
    grad[...] = before[...] + gradient(out[...], upstream[low - HALO : high - HALO, :])
    quarter = g0.shape[0]
    g0[...] = grad[pl.ds(pl.multiple_of(ids[2] * quarter, 8), quarter), :]
    for k, g in ((1, g1), (2, g2), (3, g3)):
        at = pl.multiple_of((ids[2] ^ k) * quarter, 8)
        g[...] = grad[pl.ds(at, quarter), :].astype(jnp.bfloat16)


def decode(front_rows, back_rows, weights, out):
    cut = front_rows.shape[0]
    for part, first in ((front_rows, 0), (back_rows, cut)):
        value = jnp.dot(part[...], weights[...], preferred_element_type=jnp.float32)
        out[first : first + part.shape[0], :] = value.astype(jnp.bfloat16)


def assemble(ids, p0, p1, p2, p3, out):
    quarter = p0.shape[0]
    for k, p in enumerate((p0, p1, p2, p3)):
        at = pl.multiple_of((ids[2] ^ k) * quarter, 8)
        out[pl.ds(at, quarter), :] = p[...].astype(jnp.float32)


def tie(value, *done):
    return lax.optimization_barrier((value, *done))[0]


def pairs(size, partner):
    return [(i, partner(i)) for i in range(size)]


def call(name, kernel, outs, in_specs, scratch=(), flops=0, megabytes=40):
    many = isinstance(outs, (list, tuple))
    return pl.pallas_call(
        kernel,
        out_shape=tuple(outs) if many else outs,
        in_specs=in_specs,
        out_specs=(VMEM,) * len(outs) if many else VMEM,
        scratch_shapes=list(scratch),
        compiler_params=pltpu.CompilerParams(vmem_limit_bytes=megabytes * 2**20),
        cost_estimate=pl.CostEstimate(flops=flops, bytes_accessed=2**20, transcendentals=0),
        name=name,
    )


def body(zs, seq_count, bases, stem, gains, conv_weight, dec_weight, upstream):
    bins, width = upstream.shape[1], upstream.shape[2]
    rows = bins + 2 * HALO
    count = bins * seq_count
    bf16, f32 = jnp.bfloat16, jnp.float32
    seq, chan = lax.axis_index("seq"), lax.axis_index("chan")
    x, z = seq // zs, seq % zs
    x_half, z_half = ((x + 1) // 2) % 2, ((z + 1) // 2) % 2
    ids = jnp.stack([chan, seq, x_half * 2 + z_half]).astype(jnp.int32)

    across = functools.partial(lax.ppermute, axis_name="chan", perm=pairs(4, lambda i: i ^ 2))
    other_core = functools.partial(lax.ppermute, axis_name="chan", perm=pairs(4, lambda i: i ^ 1))
    far = functools.partial(
        lax.ppermute, axis_name=("section", "chan"), perm=pairs(8, lambda i: i ^ 6)
    )

    letters = lax.optimization_barrier(bases.reshape(bins, PATCH).astype(bf16))
    up = [(i, i + 1) for i in range(seq_count - 1)]
    down = [(j, i) for i, j in up]
    half = stem.shape[0] // 2
    stem_a, stem_b = lax.optimization_barrier((stem[:half], stem[half:]))
    w2a = across(stem_a)
    w2b = far(stem_b)
    w1 = other_core(stem)
    before = lax.ppermute(letters[bins - HALO :], "seq", up)
    after = lax.ppermute(letters[:HALO], "seq", down)
    w2a, before, after = lax.optimization_barrier((w2a, before, after))
    w3a = other_core(w2a)
    w3b = other_core(w2b)
    layer_weights = jax.ShapeDtypeStruct((3, 4 * width, width), bf16)
    weight_sems = pltpu.SemaphoreType.DMA((3, 4))
    onehot, weights = call(
        "one_hot",
        functools.partial(one_hot, bins, count),
        [jax.ShapeDtypeStruct((rows, 4 * PATCH), bf16), layer_weights],
        [SMEM] + [VMEM] * 3 + [HBM],
        [weight_sems],
        flops=10**9,
    )(ids, before, letters, after, conv_weight)

    def shape(n):
        return jax.ShapeDtypeStruct((n, width), bf16)

    def work(n):
        return 2 * n * 3 * 4 * width * width

    def normed(n):
        return pltpu.VMEM((n + 2 * PAD, 4 * width), bf16)

    def exchange(own):
        return own, other_core(own), across(own)

    def finish(sent, *done):
        own, beside, remote = sent
        remote = tie(remote, *done)
        return own, beside, remote, other_core(remote)

    cut = bins // 2 + 3 * HALO
    inputs = (onehot, stem_a, stem_b, w1, w2a, w2b, w3a, w3b, gains, weights)
    part = call(
        "zero_front",
        functools.partial(first_layer, (0, cut), bins, count),
        shape(cut),
        [SMEM] + [VMEM] * 10,
        [normed(cut + HALO), pltpu.VMEM((cut + HALO, 4 * width), bf16)],
        flops=work(cut),
    )(ids, *inputs)
    sent_front = exchange(part)
    part, weights = call(
        "zero_back",
        functools.partial(first_layer, (cut, rows), bins, count),
        [shape(rows - cut), layer_weights],
        [SMEM] + [VMEM] * 10 + [HBM],
        [normed(rows - cut + HALO), pltpu.VMEM((rows - cut + HALO, 4 * width), bf16), weight_sems],
        flops=work(rows - cut),
    )(ids, *inputs, conv_weight)
    sent_back = exchange(part)
    fronts = finish(sent_front, part)

    cut = cut - HALO
    part = call(
        "one_front",
        functools.partial(front, 1, 2 * FIRST_DILATION0, (0, cut), bins, count),
        shape(cut),
        [SMEM] + [VMEM] * 6,
        [normed(cut + HALO)],
        flops=work(cut),
    )(ids, *fronts, gains, weights)
    sent_front = exchange(part)
    backs = finish(sent_back, part)
    part, weights = call(
        "one_back",
        functools.partial(back, 1, 2 * FIRST_DILATION0, (cut, rows), bins, count),
        [shape(rows - cut), layer_weights],
        [SMEM] + [VMEM] * 10 + [HBM],
        [normed(rows - cut + HALO), weight_sems],
        flops=work(rows - cut),
    )(ids, *fronts, *backs, gains, weights, conv_weight)
    sent_back = exchange(part)
    fronts = finish(sent_front, part)

    cut = cut - HALO
    front_rows, front_grad = call(
        "two_front",
        functools.partial(last_front, (HALO, cut), bins),
        [shape(cut - HALO), jax.ShapeDtypeStruct((width, width), f32)],
        [SMEM] + [VMEM] * 7,
        [normed(cut + HALO)],
        flops=work(cut - HALO),
    )(ids, *fronts, gains, weights, upstream[0])
    backs = finish(sent_back, front_rows)
    back_rows, g0, g1, g2, g3 = call(
        "two_back",
        functools.partial(last_back, (cut, rows - HALO), bins),
        [shape(rows - HALO - cut), jax.ShapeDtypeStruct((width // 4, width), f32)]
        + [shape(width // 4)] * 3,
        [SMEM] + [VMEM] * 12,
        [normed(rows - cut + HALO), pltpu.VMEM((width, width), f32)],
        flops=work(rows - HALO - cut),
    )(ids, *fronts, *backs, gains, weights, upstream[0], front_grad)
    decoded = call(
        "decode",
        decode,
        shape(bins),
        [VMEM] * 3,
        flops=2 * bins * width * width,
        megabytes=8,
    )(front_rows, back_rows, dec_weight)

    def over(fx, fz):
        def partner(i):
            return fx(i // zs) * zs + fz(i % zs)

        return functools.partial(lax.ppermute, axis_name="seq", perm=pairs(seq_count, partner))

    def same(i):
        return i

    def flip(i):
        return i ^ 1

    def xs_near(i):
        return 3 - i

    def zs_near(i):
        return (i + 1) % zs if i % 2 else (i - 1) % zs

    def zs_far(i):
        return {0: 3, 3: 0, 1: 6, 6: 1, 2: 5, 5: 2, 4: 7, 7: 4}[i]

    r2 = over(flip, same)(g2)
    r1 = over(same, flip)(g1)
    r3 = over(flip, flip)(g3)
    total = (g0 + r2.astype(f32)) + (r1.astype(f32) + r3.astype(f32))
    own = total.astype(bf16)
    rx = over(xs_near, same)(own)
    rz = over(same, zs_near)(own)
    rxz = over(xs_near, zs_near)(own)
    total = (own.astype(f32) + rx.astype(f32)) + (rz.astype(f32) + rxz.astype(f32))
    own = total.astype(bf16)
    other = lax.ppermute(own, "section", [(0, 1), (1, 0)])
    own = (own.astype(f32) + other.astype(f32)).astype(bf16)
    other = over(same, zs_far)(own)
    own = (own.astype(f32) + other.astype(f32)).astype(bf16)
    r2 = over(flip, same)(own)
    r1 = over(same, flip)(own)
    r3 = over(flip, flip)(own)
    weight_grad = call(
        "assemble",
        assemble,
        jax.ShapeDtypeStruct((width, width), f32),
        [SMEM] + [VMEM] * 4,
        megabytes=8,
    )(ids, own, r1, r2, r3)
    return (decoded[None], weight_grad)


def solution(mesh):
    placed = (
        P("section", "seq"),
        P(None, "chan"),
        P(),
        P(None, None, None, "chan"),
        P("chan", None),
        P("section", "seq", "chan"),
    )
    seq_count = mesh.shape["seq"]
    return jax.shard_map(
        functools.partial(body, seq_count // 4, seq_count),
        mesh=mesh,
        in_specs=placed,
        out_specs=(P("section", "seq", "chan"), P("chan", None)),
        check_vma=False,
    )
```

```python
import functools

import jax
import jax.numpy as jnp
from jax import lax
from jax.experimental import pallas as pl
from jax.experimental.pallas import tpu as pltpu
from jax.sharding import PartitionSpec as P

PATCH = 128
FIRST_DILATION0 = 2
EPSILON = 1e-06
HALO = 16
STEP = 32
PAD = 16

VMEM = pl.BlockSpec(memory_space=pltpu.VMEM)
SMEM = pl.BlockSpec(memory_space=pltpu.SMEM)
HBM = pl.BlockSpec(memory_space=pltpu.HBM)


def gelu(x):
    inner = x * (0.7978845608028654 + 0.035677408136300125 * (x * x))
    return (0.5 * x) * (1.0 + jnp.tanh(inner))


def in_sequence(ids, first, rows, bins, count):
    bin_at = lax.broadcasted_iota(jnp.int32, (rows, 1), 0) + (ids[1] * bins - HALO + first)
    return jnp.where((bin_at >= 0) & (bin_at < count), 1.0, 0.0)


def norm_rows(ids, layer, pieces, gains, normed, at):
    rows, width = pieces[0].shape
    wide = [p.astype(jnp.float32) for p in pieces]
    total = wide[0] * wide[0]
    for w in wide[1:]:
        total = total + w * w
    inverse = lax.rsqrt(jnp.sum(total, axis=-1, keepdims=True) * (1.0 / (4 * width)) + EPSILON)
    for k, w in enumerate(wide):
        at_lane = pl.multiple_of((ids[0] ^ k) * width, 128)
        value = gelu(w * inverse * gains[layer : layer + 1, pl.ds(at_lane, width)])
        normed[at : at + rows, k * width : (k + 1) * width] = value.astype(jnp.bfloat16)


def norm_segment(ids, layer, read, count, gains, normed, at):
    for first in range(0, count, STEP):
        rows = min(STEP, count - first)
        norm_rows(ids, layer, read(first, rows), gains, normed, at + first)


def convolve(normed, weights, at, rows, dilation):
    update = None
    for t in range(3):
        first = at + (t - 1) * dilation
        part = jnp.dot(
            normed[first : first + rows, :], weights[t][...], preferred_element_type=jnp.float32
        )
        update = part if update is None else update + part
    return update


def clear(ref, first, rows):
    ref[first : first + rows, :] = jnp.zeros((rows, ref.shape[1]), ref.dtype)


def start_weights(ids, layer, taps, w_hbm, outs, sems):
    copies = []
    for n, (t, out) in enumerate(zip(taps, outs)):
        width = out.shape[1]
        for k in range(4):
            copies.append(
                pltpu.make_async_copy(
                    w_hbm.at[layer, t, pl.ds((ids[0] ^ k) * width, width), :],
                    out.at[pl.ds(k * width, width), :],
                    sems.at[n, k],
                )
            )
            copies[-1].start()
    return copies


def wait_all(copies):
    for copy in copies:
        copy.wait()


def one_hot(bins, count, ids, before, own, after, w_hbm, onehot, *refs):
    copies = start_weights(ids, 0, range(3), w_hbm, refs[:3], refs[3])
    letters = jnp.concatenate([before[...], own[...], after[...]], axis=0)
    lane = lax.broadcasted_iota(jnp.int32, (PATCH, 4 * PATCH), 1)
    row = lax.broadcasted_iota(jnp.int32, (PATCH, 4 * PATCH), 0)
    spread = jnp.where(lane // 4 == row, 1.0, 0.0).astype(jnp.bfloat16)
    repeated = jnp.dot(letters, spread, preferred_element_type=jnp.float32)
    base = (lax.broadcasted_iota(jnp.int32, (1, 4 * PATCH), 1) % 4).astype(jnp.float32)
    inside = in_sequence(ids, 0, bins + 2 * HALO, bins, count)
    onehot[...] = (jnp.where(repeated == base, 1.0, 0.0) * inside).astype(jnp.bfloat16)
    wait_all(copies)


def fetching(kernel, inputs, results, layer, taps):
    def run(ids, *refs):
        ins, (w_hbm, *refs) = refs[:inputs], refs[inputs:]
        outs, later, refs = refs[:results], refs[results : results + len(taps)], refs[results + len(taps) :]
        copies = start_weights(ids, layer, taps, w_hbm, later, refs[-1])
        kernel(ids, *ins, *outs, *refs[:-1])
        wait_all(copies)

    return run


def first_layer(span, bins, count, ids, onehot, own_a, own_b, w1, w2a, w2b, w3a, w3b, gains, *refs):
    low, high = span
    weights, (out, normed, stream) = refs[:3], refs[3:]
    width = out.shape[1]
    first, last = max(low - HALO, 0), min(high + HALO, bins + 2 * HALO)
    rows = last - first
    clear(normed, 0, PAD)
    clear(normed, PAD + rows, PAD)
    stem = jnp.concatenate(
        [
            jnp.concatenate([own_a[...], own_b[...]], axis=0),
            w1[...],
            jnp.concatenate([w2a[...], w2b[...]], axis=0),
            jnp.concatenate([w3a[...], w3b[...]], axis=0),
        ],
        axis=1,
    )
    stream[...] = jnp.dot(
        onehot[first:last, :], stem, preferred_element_type=jnp.float32
    ).astype(jnp.bfloat16)

    def read(at, n):
        return [stream[at : at + n, k * width : (k + 1) * width] for k in range(4)]

    norm_segment(ids, 0, read, rows, gains, normed, PAD)
    update = convolve(normed, weights, PAD + low - first, high - low, FIRST_DILATION0)
    total = stream[low - first : high - first, 0:width].astype(jnp.float32) + update
    inside = in_sequence(ids, low, high - low, bins, count)
    out[...] = (total * inside).astype(jnp.bfloat16)


def front(layer, dilation, span, bins, count, ids, *refs):
    pieces, gains, weights, (out, normed) = refs[:4], refs[4], refs[5:8], refs[8:]
    low, high = span
    rows = high + HALO
    clear(normed, 0, PAD)

    def read(at, n):
        return [p[at : at + n, :] for p in pieces]

    norm_segment(ids, layer, read, rows, gains, normed, PAD)
    update = convolve(normed, weights, PAD + low, high - low, dilation)
    total = pieces[0][low:high, :].astype(jnp.float32) + update
    if count:
        total = total * in_sequence(ids, low, high - low, bins, count)
    out[...] = total.astype(jnp.bfloat16)


def back(layer, dilation, span, bins, count, ids, *refs):
    fronts, backs, gains, weights, (out, normed) = refs[:4], refs[4:8], refs[8], refs[9:12], refs[12:]
    low, high = span
    first = low - HALO
    joint = fronts[0].shape[0]
    rows = joint + backs[0].shape[0] - first
    clear(normed, PAD + rows, PAD)

    def read_front(at, n):
        return [p[first + at : first + at + n, :] for p in fronts]

    def read_back(at, n):
        return [p[at : at + n, :] for p in backs]

    norm_segment(ids, layer, read_front, joint - first, gains, normed, PAD)
    norm_segment(ids, layer, read_back, backs[0].shape[0], gains, normed, PAD + joint - first)
    update = convolve(normed, weights, PAD + HALO, high - low, dilation)
    own = jnp.concatenate([fronts[0][low:joint, :], backs[0][0 : high - joint, :]], axis=0)
    total = own.astype(jnp.float32) + update
    if count:
        total = total * in_sequence(ids, low, high - low, bins, count)
    out[...] = total.astype(jnp.bfloat16)


def gradient(stream, upstream):
    return lax.dot_general(
        stream, upstream, (((0,), (0,)), ((), ())), preferred_element_type=jnp.float32
    )


def last_front(span, bins, ids, *refs):
    refs, (upstream, out, grad, normed) = refs[:8], refs[8:]
    front(2, 4 * FIRST_DILATION0, span, bins, 0, ids, *refs, out, normed)
    low, high = span
    grad[...] = gradient(out[...], upstream[low - HALO : high - HALO, :])


def last_back(span, bins, ids, *refs):
    refs, (upstream, before, out, g0, g1, g2, g3, normed, grad) = refs[:12], refs[12:]
    back(2, 4 * FIRST_DILATION0, span, bins, 0, ids, *refs, out, normed)
    low, high = span
    grad[...] = before[...] + gradient(out[...], upstream[low - HALO : high - HALO, :])
    quarter = g0.shape[0]
    for k, g in enumerate((g0, g1, g2, g3)):
        g[...] = grad[pl.ds(quarter_at(ids, k, quarter), quarter), :].astype(g.dtype)


def quarter_at(ids, k, quarter):
    return pl.multiple_of((ids[2] ^ (ids[2 + k] if k else 0)) * quarter, 8)


def decode(front_rows, back_rows, weights, out):
    cut = front_rows.shape[0]
    for part, first in ((front_rows, 0), (back_rows, cut)):
        value = jnp.dot(part[...], weights[...], preferred_element_type=jnp.float32)
        out[first : first + part.shape[0], :] = value.astype(jnp.bfloat16)


def assemble(ids, p0, p1, p2, p3, out):
    quarter = p0.shape[0]
    for k, p in enumerate((p0, p1, p2, p3)):
        out[pl.ds(quarter_at(ids, k, quarter), quarter), :] = p[...].astype(jnp.float32)


def tie(value, *done):
    return lax.optimization_barrier((value, *done))[0]


def pairs(size, partner):
    return [(i, partner(i)) for i in range(size)]


def call(name, kernel, outs, in_specs, scratch=(), flops=0, megabytes=40):
    many = isinstance(outs, (list, tuple))
    return pl.pallas_call(
        kernel,
        out_shape=tuple(outs) if many else outs,
        in_specs=in_specs,
        out_specs=(VMEM,) * len(outs) if many else VMEM,
        scratch_shapes=list(scratch),
        compiler_params=pltpu.CompilerParams(vmem_limit_bytes=megabytes * 2**20),
        cost_estimate=pl.CostEstimate(flops=flops, bytes_accessed=2**20, transcendentals=0),
        name=name,
    )


def body(zs, seq_count, bases, stem, gains, conv_weight, dec_weight, upstream):
    bins, width = upstream.shape[1], upstream.shape[2]
    rows = bins + 2 * HALO
    count = bins * seq_count
    bf16, f32 = jnp.bfloat16, jnp.float32
    seq, chan = lax.axis_index("seq"), lax.axis_index("chan")
    x, z = seq // zs, seq % zs
    x_half, z_half = ((x + 1) // 2) % 2, ((z + 1) // 2) % 2
    core = chan % 2
    ids = jnp.stack([chan, seq, x_half * 2 + z_half, 2 - core, 1 + core, 3 + 0 * core])
    ids = ids.astype(jnp.int32)

    across = functools.partial(lax.ppermute, axis_name="chan", perm=pairs(4, lambda i: i ^ 2))
    other_core = functools.partial(lax.ppermute, axis_name="chan", perm=pairs(4, lambda i: i ^ 1))
    far = functools.partial(
        lax.ppermute, axis_name=("section", "chan"), perm=pairs(8, lambda i: i ^ 6)
    )

    letters = bases.reshape(bins, PATCH)
    up = [(i, i + 1) for i in range(seq_count - 1)]
    down = [(j, i) for i, j in up]
    half = stem.shape[0] // 2
    stem_a, stem_b = lax.optimization_barrier((stem[:half], stem[half:]))
    w2a = across(stem_a)
    w2b = far(stem_b)
    w1 = other_core(stem)
    before = lax.ppermute(letters[bins - HALO :].astype(bf16), "seq", up)
    after = lax.ppermute(letters[:HALO].astype(bf16), "seq", down)
    letters = lax.optimization_barrier(letters.astype(bf16))
    w2a, before, after = lax.optimization_barrier((w2a, before, after))
    w3a = other_core(w2a)
    w3b = other_core(w2b)
    tap = jax.ShapeDtypeStruct((4 * width, width), bf16)
    tap_sems = pltpu.SemaphoreType.DMA((3, 4))
    onehot, *weights = call(
        "one_hot",
        functools.partial(one_hot, bins, count),
        [jax.ShapeDtypeStruct((rows, 4 * PATCH), bf16)] + [tap] * 3,
        [SMEM] + [VMEM] * 3 + [HBM],
        [tap_sems],
        flops=10**9,
    )(ids, before, letters, after, conv_weight)

    def shape(n):
        return jax.ShapeDtypeStruct((n, width), bf16)

    def work(n):
        return 2 * n * 3 * 4 * width * width

    def normed(n):
        return pltpu.VMEM((n + 2 * PAD, 4 * width), bf16)

    def exchange(own):
        return own, other_core(own), across(own)

    def finish(sent, *done):
        own, beside, remote = sent
        remote = tie(remote, *done)
        return own, beside, remote, other_core(remote)

    cut = bins // 2 + 3 * HALO
    inputs = (onehot, stem_a, stem_b, w1, w2a, w2b, w3a, w3b, gains, *weights)
    part, tap0 = call(
        "zero_front",
        fetching(functools.partial(first_layer, (0, cut), bins, count), 12, 1, 1, (0,)),
        [shape(cut), tap],
        [SMEM] + [VMEM] * 12 + [HBM],
        [normed(cut + HALO), pltpu.VMEM((cut + HALO, 4 * width), bf16), tap_sems],
        flops=work(cut),
    )(ids, *inputs, conv_weight)
    sent_front = exchange(part)
    part, *taps = call(
        "zero_back",
        fetching(functools.partial(first_layer, (cut, rows), bins, count), 12, 1, 1, (1, 2)),
        [shape(rows - cut), tap, tap],
        [SMEM] + [VMEM] * 12 + [HBM],
        [normed(rows - cut + HALO), pltpu.VMEM((rows - cut + HALO, 4 * width), bf16), tap_sems],
        flops=work(rows - cut),
    )(ids, *inputs, conv_weight)
    weights = (tap0, *taps)
    sent_back = exchange(part)
    fronts = finish(sent_front, part)

    cut = cut - HALO
    layer = (1, 2 * FIRST_DILATION0)
    part, tap0 = call(
        "one_front",
        fetching(functools.partial(front, *layer, (0, cut), bins, count), 8, 1, 2, (0,)),
        [shape(cut), tap],
        [SMEM] + [VMEM] * 8 + [HBM],
        [normed(cut + HALO), tap_sems],
        flops=work(cut),
    )(ids, *fronts, gains, *weights, conv_weight)
    sent_front = exchange(part)
    backs = finish(sent_back, part)
    part, *taps = call(
        "one_back",
        fetching(functools.partial(back, *layer, (cut, rows), bins, count), 12, 1, 2, (1, 2)),
        [shape(rows - cut), tap, tap],
        [SMEM] + [VMEM] * 12 + [HBM],
        [normed(rows - cut + HALO), tap_sems],
        flops=work(rows - cut),
    )(ids, *fronts, *backs, gains, *weights, conv_weight)
    weights = (tap0, *taps)
    sent_back = exchange(part)
    fronts = finish(sent_front, part)

    cut = cut - HALO
    front_rows, front_grad = call(
        "two_front",
        functools.partial(last_front, (HALO, cut), bins),
        [shape(cut - HALO), jax.ShapeDtypeStruct((width, width), f32)],
        [SMEM] + [VMEM] * 9,
        [normed(cut + HALO)],
        flops=work(cut - HALO),
    )(ids, *fronts, gains, *weights, upstream[0])
    backs = finish(sent_back, front_rows)
    back_rows, g0, g1, g2, g3 = call(
        "two_back",
        functools.partial(last_back, (cut, rows - HALO), bins),
        [shape(rows - HALO - cut), jax.ShapeDtypeStruct((width // 4, width), f32)]
        + [shape(width // 4)] * 3,
        [SMEM] + [VMEM] * 14,
        [normed(rows - cut + HALO), pltpu.VMEM((width, width), f32)],
        flops=work(rows - HALO - cut),
    )(ids, *fronts, *backs, gains, *weights, upstream[0], front_grad)
    decoded = call(
        "decode",
        decode,
        shape(bins),
        [VMEM] * 3,
        flops=2 * bins * width * width,
        megabytes=8,
    )(front_rows, back_rows, dec_weight)


    def same(i):
        return i

    def flip(i):
        return i ^ 1

    def xs_near(i):
        return 3 - i

    def zs_near(i):
        return (i + 1) % zs if i % 2 else (i - 1) % zs

    def zs_far(i):
        return {0: 3, 3: 0, 1: 6, 6: 1, 2: 5, 5: 2, 4: 7, 7: 4}[i]

    def swap(own, *moves):
        def partner(i):
            pair, lane = divmod(i, 4)
            section, spot = divmod(pair, seq_count)
            fs, fx, fz = moves[lane % len(moves)]
            spot = fx(spot // zs) * zs + fz(spot % zs)
            return (fs(section) * seq_count + spot) * 4 + lane

        perm = pairs(2 * seq_count * 4, partner)
        return lax.ppermute(own, ("section", "seq", "chan"), perm)

    def swap_three(fx, fz, a, b, c):
        both = swap(c, (same, fx, fz))
        along_x, along_z = (same, fx, same), (same, same, fz)
        return swap(a, along_x, along_z), swap(b, along_z, along_x), both

    def add(a, b):
        return (a.astype(f32) + b.astype(f32)).astype(bf16)

    r1, r2, r3 = swap_three(flip, flip, g1, g2, g3)
    total = (g0 + r1.astype(f32)) + (r2.astype(f32) + r3.astype(f32))
    own = total.astype(bf16)
    r1, r2, r3 = swap_three(xs_near, zs_near, own, own, own)
    total = (own.astype(f32) + r1.astype(f32)) + (r2.astype(f32) + r3.astype(f32))
    own = total.astype(bf16)
    sections, far_z = (flip, same, same), (same, same, zs_far)
    own = add(own, swap(own, sections, far_z))
    own = add(own, swap(own, far_z, sections))
    r1, r2, r3 = swap_three(flip, flip, own, own, own)
    weight_grad = call(
        "assemble",
        assemble,
        jax.ShapeDtypeStruct((width, width), f32),
        [SMEM] + [VMEM] * 4,
        megabytes=8,
    )(ids, own, r1, r2, r3)
    return (decoded[None], weight_grad)


def solution(mesh):
    placed = (
        P("section", "seq"),
        P(None, "chan"),
        P(),
        P(None, None, None, "chan"),
        P("chan", None),
        P("section", "seq", "chan"),
    )
    seq_count = mesh.shape["seq"]
    return jax.shard_map(
        functools.partial(body, seq_count // 4, seq_count),
        mesh=mesh,
        in_specs=placed,
        out_specs=(P("section", "seq", "chan"), P("chan", None)),
        check_vma=False,
    )
```

```python
import functools

import jax
import jax.numpy as jnp
from jax import lax
from jax.experimental import pallas as pl
from jax.experimental.pallas import tpu as pltpu
from jax.sharding import PartitionSpec as P

PATCH = 128
FIRST_DILATION0 = 2
EPSILON = 1e-06
HALO = 16
STEP = 32
PAD = 16

VMEM = pl.BlockSpec(memory_space=pltpu.VMEM)
SMEM = pl.BlockSpec(memory_space=pltpu.SMEM)
HBM = pl.BlockSpec(memory_space=pltpu.HBM)


def gelu(x):
    inner = x * (0.7978845608028654 + 0.035677408136300125 * (x * x))
    return (0.5 * x) * (1.0 + jnp.tanh(inner))


def in_sequence(ids, first, rows, bins, count):
    bin_at = lax.broadcasted_iota(jnp.int32, (rows, 1), 0) + (ids[1] * bins - HALO + first)
    return jnp.where((bin_at >= 0) & (bin_at < count), 1.0, 0.0)


def norm_rows(ids, layer, pieces, gains, normed, at):
    rows, width = pieces[0].shape
    wide = [p.astype(jnp.float32) for p in pieces]
    total = wide[0] * wide[0]
    for w in wide[1:]:
        total = total + w * w
    inverse = lax.rsqrt(jnp.sum(total, axis=-1, keepdims=True) * (1.0 / (4 * width)) + EPSILON)
    for k, w in enumerate(wide):
        at_lane = pl.multiple_of((ids[0] ^ k) * width, 128)
        value = gelu(w * inverse * gains[layer : layer + 1, pl.ds(at_lane, width)])
        normed[at : at + rows, k * width : (k + 1) * width] = value.astype(jnp.bfloat16)


def norm_segment(ids, layer, read, count, gains, normed, at):
    for first in range(0, count, STEP):
        rows = min(STEP, count - first)
        norm_rows(ids, layer, read(first, rows), gains, normed, at + first)


def convolve(normed, weights, at, rows, dilation):
    update = None
    for t in range(3):
        first = at + (t - 1) * dilation
        part = jnp.dot(
            normed[first : first + rows, :], weights[t], preferred_element_type=jnp.float32
        )
        update = part if update is None else update + part
    return update


def clear(ref, first, rows):
    ref[first : first + rows, :] = jnp.zeros((rows, ref.shape[1]), ref.dtype)


def one_hot(letters):
    letters = letters.astype(jnp.float32).astype(jnp.bfloat16)
    lane = lax.broadcasted_iota(jnp.int32, (PATCH, 4 * PATCH), 1)
    row = lax.broadcasted_iota(jnp.int32, (PATCH, 4 * PATCH), 0)
    spread = jnp.where(lane // 4 == row, 1.0, 0.0).astype(jnp.bfloat16)
    repeated = jnp.dot(letters, spread, preferred_element_type=jnp.float32)
    base = (lax.broadcasted_iota(jnp.int32, (1, 4 * PATCH), 1) % 4).astype(jnp.float32)
    return jnp.where(repeated == base, 1.0, 0.0).astype(jnp.bfloat16)


def fetch(layer, ids, w_hbm, weights, sems):
    width = weights.shape[2]
    copies = []
    for t in range(3):
        for k in range(4):
            copies.append(
                pltpu.make_async_copy(
                    w_hbm.at[layer, t, pl.ds((ids[0] ^ k) * width, width), :],
                    weights.at[t, pl.ds(k * width, width), :],
                    sems.at[t, k],
                )
            )
            copies[-1].start()
    for copy in copies:
        copy.wait()


def prepare(letters, onehot):
    onehot[...] = one_hot(letters[...])


def first_layer(span, bins, count, ids, onehot, halo, own_a, own_b, w1, w2a, w2b, w3a, w3b, gains, weights, out, normed, stream):
    low, high = span
    width = out.shape[1]
    first, last = max(low - HALO, 0), min(high + HALO, bins + 2 * HALO)
    rows = last - first
    clear(normed, 0, PAD)
    clear(normed, PAD + rows, PAD)
    stem = jnp.concatenate(
        [
            jnp.concatenate([own_a[...], own_b[...]], axis=0),
            w1[...],
            jnp.concatenate([w2a[...], w2b[...]], axis=0),
            jnp.concatenate([w3a[...], w3b[...]], axis=0),
        ],
        axis=1,
    )
    beyond = one_hot(halo[...])
    if low == 0:
        beyond = jnp.where(ids[1] > 0, beyond, jnp.zeros_like(beyond))
        lines = jnp.concatenate([beyond, onehot[0 : last - HALO, :]], axis=0)
    else:
        beyond = jnp.where((ids[1] + 1) * bins < count, beyond, jnp.zeros_like(beyond))
        lines = jnp.concatenate([onehot[first - HALO : bins, :], beyond], axis=0)
    stream[...] = jnp.dot(lines, stem, preferred_element_type=jnp.float32).astype(jnp.bfloat16)

    def read(at, n):
        return [stream[at : at + n, k * width : (k + 1) * width] for k in range(4)]

    norm_segment(ids, 0, read, rows, gains, normed, PAD)
    update = convolve(normed, weights, PAD + low - first, high - low, FIRST_DILATION0)
    total = stream[low - first : high - first, 0:width].astype(jnp.float32) + update
    inside = in_sequence(ids, low, high - low, bins, count)
    out[...] = (total * inside).astype(jnp.bfloat16)


def front(layer, dilation, span, bins, count, ids, *refs):
    pieces, (gains, weights, out, normed) = refs[:4], refs[4:]
    low, high = span
    rows = high + HALO
    clear(normed, 0, PAD)

    def read(at, n):
        return [p[at : at + n, :] for p in pieces]

    norm_segment(ids, layer, read, rows, gains, normed, PAD)
    update = convolve(normed, weights, PAD + low, high - low, dilation)
    total = pieces[0][low:high, :].astype(jnp.float32) + update
    if count:
        total = total * in_sequence(ids, low, high - low, bins, count)
    out[...] = total.astype(jnp.bfloat16)


def back(layer, dilation, span, bins, count, ids, *refs):
    fronts, backs, (gains, weights, out, normed) = refs[:4], refs[4:8], refs[8:]
    low, high = span
    first = low - HALO
    joint = fronts[0].shape[0]
    rows = joint + backs[0].shape[0] - first
    clear(normed, PAD + rows, PAD)

    def read_front(at, n):
        return [p[first + at : first + at + n, :] for p in fronts]

    def read_back(at, n):
        return [p[at : at + n, :] for p in backs]

    norm_segment(ids, layer, read_front, joint - first, gains, normed, PAD)
    norm_segment(ids, layer, read_back, backs[0].shape[0], gains, normed, PAD + joint - first)
    update = convolve(normed, weights, PAD + HALO, high - low, dilation)
    own = jnp.concatenate([fronts[0][low:joint, :], backs[0][0 : high - joint, :]], axis=0)
    total = own.astype(jnp.float32) + update
    if count:
        total = total * in_sequence(ids, low, high - low, bins, count)
    out[...] = total.astype(jnp.bfloat16)


def gradient(stream, upstream):
    return lax.dot_general(
        stream, upstream, (((0,), (0,)), ((), ())), preferred_element_type=jnp.float32
    )


def last_front(span, bins, ids, *refs):
    refs, (upstream, out, grad, normed) = refs[:6], refs[6:]
    front(2, 4 * FIRST_DILATION0, span, bins, 0, ids, *refs, out, normed)
    low, high = span
    grad[...] = gradient(out[...], upstream[low - HALO : high - HALO, :])


def last_back(span, bins, ids, *refs):
    refs, (upstream, before, out, g0, g1, g2, g3, normed, grad) = refs[:10], refs[10:]
    back(2, 4 * FIRST_DILATION0, span, bins, 0, ids, *refs, out, normed)
    low, high = span
    grad[...] = before[...] + gradient(out[...], upstream[low - HALO : high - HALO, :])
    quarter = g0.shape[0]
    for k, g in enumerate((g0, g1, g2, g3)):
        g[...] = grad[pl.ds(quarter_at(ids, k, quarter), quarter), :].astype(g.dtype)


def quarter_at(ids, k, quarter):
    return pl.multiple_of((ids[2] ^ (ids[2 + k] if k else 0)) * quarter, 8)


def decode(front_rows, back_rows, weights, out):
    cut = front_rows.shape[0]
    for part, first in ((front_rows, 0), (back_rows, cut)):
        value = jnp.dot(part[...], weights[...], preferred_element_type=jnp.float32)
        out[first : first + part.shape[0], :] = value.astype(jnp.bfloat16)


def assemble(ids, p0, p1, p2, p3, out):
    quarter = p0.shape[0]
    for k, p in enumerate((p0, p1, p2, p3)):
        out[pl.ds(quarter_at(ids, k, quarter), quarter), :] = p[...].astype(jnp.float32)


def tie(value, *done):
    return lax.optimization_barrier((value, *done))[0]


def pairs(size, partner):
    return [(i, partner(i)) for i in range(size)]


def call(name, kernel, outs, in_specs, scratch=(), flops=0, megabytes=46):
    many = isinstance(outs, (list, tuple))
    return pl.pallas_call(
        kernel,
        out_shape=tuple(outs) if many else outs,
        in_specs=in_specs,
        out_specs=(VMEM,) * len(outs) if many else VMEM,
        scratch_shapes=list(scratch),
        compiler_params=pltpu.CompilerParams(vmem_limit_bytes=megabytes * 2**20),
        cost_estimate=pl.CostEstimate(flops=flops, bytes_accessed=2**20, transcendentals=0),
        name=name,
    )


def body(zs, seq_count, bases, stem, gains, conv_weight, dec_weight, upstream):
    bins, width = upstream.shape[1], upstream.shape[2]
    rows = bins + 2 * HALO
    count = bins * seq_count
    bf16, f32 = jnp.bfloat16, jnp.float32
    seq, chan = lax.axis_index("seq"), lax.axis_index("chan")
    x, z = seq // zs, seq % zs
    x_half, z_half = ((x + 1) // 2) % 2, ((z + 1) // 2) % 2
    core = chan % 2
    ids = jnp.stack([chan, seq, x_half * 2 + z_half, 2 - core, 1 + core, 3 + 0 * core])
    ids = ids.astype(jnp.int32)

    across = functools.partial(lax.ppermute, axis_name="chan", perm=pairs(4, lambda i: i ^ 2))
    other_core = functools.partial(lax.ppermute, axis_name="chan", perm=pairs(4, lambda i: i ^ 1))
    far = functools.partial(
        lax.ppermute, axis_name=("section", "chan"), perm=pairs(8, lambda i: i ^ 6)
    )

    letters = bases.reshape(bins, PATCH)
    up = [(i, i + 1) for i in range(seq_count - 1)]
    down = [(j, i) for i, j in up]
    half = stem.shape[0] // 2
    stem_a, stem_b = lax.optimization_barrier((stem[:half], stem[half:]))
    w2a = across(stem_a)
    w2b = far(stem_b)
    w1 = other_core(stem)
    before = lax.ppermute(letters[bins - HALO :], "seq", up)
    def fetched(layer, *done):
        return call(
            "fetch",
            functools.partial(fetch, layer),
            jax.ShapeDtypeStruct(conv_weight.shape[1:], bf16),
            [SMEM, HBM],
            [pltpu.SemaphoreType.DMA((3, 4))],
            flops=10**9,
        )(tie(ids, *done) if done else ids, conv_weight)

    onehot = call(
        "prepare",
        prepare,
        jax.ShapeDtypeStruct((bins, 4 * PATCH), bf16),
        [VMEM],
        flops=10**9,
    )(letters)
    after = lax.ppermute(letters[:HALO], "seq", down)
    weights = fetched(0)
    w2a = tie(w2a, before, after, onehot, weights)
    w3a = other_core(w2a)
    w3b = other_core(w2b)

    def shape(n):
        return jax.ShapeDtypeStruct((n, width), bf16)

    def work(n):
        return 2 * n * 3 * 4 * width * width

    def normed(n):
        return pltpu.VMEM((n + 2 * PAD, 4 * width), bf16)

    def exchange(own):
        return own, other_core(own), across(own)

    def finish(sent, *done):
        own, beside, remote = sent
        remote = tie(remote, *done)
        return own, beside, remote, other_core(remote)

    cut = bins // 2 + 3 * HALO
    inputs = (stem_a, stem_b, w1, w2a, w2b, w3a, w3b, gains, weights)
    part = call(
        "zero_front",
        functools.partial(first_layer, (0, cut), bins, count),
        shape(cut),
        [SMEM] + [VMEM] * 11,
        [normed(cut + HALO), pltpu.VMEM((cut + HALO, 4 * width), bf16)],
        flops=work(cut),
    )(ids, onehot, before, *inputs)
    sent_front = exchange(part)
    part = call(
        "zero_back",
        functools.partial(first_layer, (cut, rows), bins, count),
        shape(rows - cut),
        [SMEM] + [VMEM] * 11,
        [normed(rows - cut + HALO), pltpu.VMEM((rows - cut + HALO, 4 * width), bf16)],
        flops=work(rows - cut),
    )(ids, onehot, after, *inputs)
    sent_back = exchange(part)
    weights = fetched(1, part)
    fronts = finish(sent_front, part, weights)

    cut = cut - HALO
    layer = (1, 2 * FIRST_DILATION0)
    part = call(
        "one_front",
        functools.partial(front, *layer, (0, cut), bins, count),
        shape(cut),
        [SMEM] + [VMEM] * 6,
        [normed(cut + HALO)],
        flops=work(cut),
    )(ids, *fronts, gains, weights)
    sent_front = exchange(part)
    backs = finish(sent_back, part)
    part = call(
        "one_back",
        functools.partial(back, *layer, (cut, rows), bins, count),
        shape(rows - cut),
        [SMEM] + [VMEM] * 10,
        [normed(rows - cut + HALO)],
        flops=work(rows - cut),
    )(ids, *fronts, *backs, gains, weights)
    sent_back = exchange(part)
    weights = fetched(2, part)
    fronts = finish(sent_front, part, weights)

    cut = cut - HALO
    front_rows, front_grad = call(
        "two_front",
        functools.partial(last_front, (HALO, cut), bins),
        [shape(cut - HALO), jax.ShapeDtypeStruct((width, width), f32)],
        [SMEM] + [VMEM] * 7,
        [normed(cut + HALO)],
        flops=work(cut - HALO),
    )(ids, *fronts, gains, weights, upstream[0])
    backs = finish(sent_back, front_rows)
    back_rows, g0, g1, g2, g3 = call(
        "two_back",
        functools.partial(last_back, (cut, rows - HALO), bins),
        [shape(rows - HALO - cut), jax.ShapeDtypeStruct((width // 4, width), f32)]
        + [shape(width // 4)] * 3,
        [SMEM] + [VMEM] * 12,
        [normed(rows - cut + HALO), pltpu.VMEM((width, width), f32)],
        flops=work(rows - HALO - cut),
    )(ids, *fronts, *backs, gains, weights, upstream[0], front_grad)
    decoded = call(
        "decode",
        decode,
        shape(bins),
        [VMEM] * 3,
        flops=2 * bins * width * width,
        megabytes=8,
    )(front_rows, back_rows, dec_weight)


    def same(i):
        return i

    def flip(i):
        return i ^ 1

    def xs_near(i):
        return 3 - i

    def zs_near(i):
        return (i + 1) % zs if i % 2 else (i - 1) % zs

    def zs_far(i):
        return {0: 3, 3: 0, 1: 6, 6: 1, 2: 5, 5: 2, 4: 7, 7: 4}[i]

    def swap(own, *moves):
        def partner(i):
            pair, lane = divmod(i, 4)
            section, spot = divmod(pair, seq_count)
            fs, fx, fz = moves[lane % len(moves)]
            spot = fx(spot // zs) * zs + fz(spot % zs)
            return (fs(section) * seq_count + spot) * 4 + lane

        perm = pairs(2 * seq_count * 4, partner)
        return lax.ppermute(own, ("section", "seq", "chan"), perm)

    def swap_three(fx, fz, a, b, c):
        both = swap(c, (same, fx, fz))
        along_x, along_z = (same, fx, same), (same, same, fz)
        return swap(a, along_x, along_z), swap(b, along_z, along_x), both

    def add(a, b):
        return (a.astype(f32) + b.astype(f32)).astype(bf16)

    r1, r2, r3 = swap_three(flip, flip, g1, g2, g3)
    total = (g0 + r1.astype(f32)) + (r2.astype(f32) + r3.astype(f32))
    own = total.astype(bf16)
    r1, r2, r3 = swap_three(xs_near, zs_near, own, own, own)
    total = (own.astype(f32) + r1.astype(f32)) + (r2.astype(f32) + r3.astype(f32))
    own = total.astype(bf16)
    sections, far_z = (flip, same, same), (same, same, zs_far)
    own = add(own, swap(own, sections, far_z))
    own = add(own, swap(own, far_z, sections))
    r1, r2, r3 = swap_three(flip, flip, own, own, own)
    weight_grad = call(
        "assemble",
        assemble,
        jax.ShapeDtypeStruct((width, width), f32),
        [SMEM] + [VMEM] * 4,
        megabytes=8,
    )(ids, own, r1, r2, r3)
    return (decoded[None], weight_grad)


def solution(mesh):
    placed = (
        P("section", "seq"),
        P(None, "chan"),
        P(),
        P(None, None, None, "chan"),
        P("chan", None),
        P("section", "seq", "chan"),
    )
    seq_count = mesh.shape["seq"]
    return jax.shard_map(
        functools.partial(body, seq_count // 4, seq_count),
        mesh=mesh,
        in_specs=placed,
        out_specs=(P("section", "seq", "chan"), P("chan", None)),
        check_vma=False,
    )
```

```python
import functools

import jax
import jax.numpy as jnp
from jax import lax
from jax.experimental import pallas as pl
from jax.experimental.pallas import tpu as pltpu
from jax.sharding import PartitionSpec as P

PATCH = 128
FIRST_DILATION0 = 2
EPSILON = 1e-06
HALO = 16
STEP = 32
PAD = 16

VMEM = pl.BlockSpec(memory_space=pltpu.VMEM)
SMEM = pl.BlockSpec(memory_space=pltpu.SMEM)
HBM = pl.BlockSpec(memory_space=pltpu.HBM)


def gelu(x):
    inner = x * (0.7978845608028654 + 0.035677408136300125 * (x * x))
    return (0.5 * x) * (1.0 + jnp.tanh(inner))


def in_sequence(ids, first, rows, bins, count):
    bin_at = lax.broadcasted_iota(jnp.int32, (rows, 1), 0) + (ids[1] * bins - HALO + first)
    return jnp.where((bin_at >= 0) & (bin_at < count), 1.0, 0.0)


def norm_rows(ids, layer, pieces, gains, normed, at):
    rows, width = pieces[0].shape
    wide = [p.astype(jnp.float32) for p in pieces]
    total = wide[0] * wide[0]
    for w in wide[1:]:
        total = total + w * w
    inverse = lax.rsqrt(jnp.sum(total, axis=-1, keepdims=True) * (1.0 / (4 * width)) + EPSILON)
    for k, w in enumerate(wide):
        at_lane = pl.multiple_of((ids[0] ^ k) * width, 128)
        value = gelu(w * inverse * gains[layer : layer + 1, pl.ds(at_lane, width)])
        normed[at : at + rows, k * width : (k + 1) * width] = value.astype(jnp.bfloat16)


def norm_segment(ids, layer, read, count, gains, normed, at):
    for first in range(0, count, STEP):
        rows = min(STEP, count - first)
        norm_rows(ids, layer, read(first, rows), gains, normed, at + first)


def convolve(normed, weights, at, rows, dilation):
    update = None
    for t in range(3):
        first = at + (t - 1) * dilation
        part = jnp.dot(
            normed[first : first + rows, :], weights[t], preferred_element_type=jnp.float32
        )
        update = part if update is None else update + part
    return update


def clear(ref, first, rows):
    ref[first : first + rows, :] = jnp.zeros((rows, ref.shape[1]), ref.dtype)


def one_hot(letters):
    letters = letters.astype(jnp.float32).astype(jnp.bfloat16)
    lane = lax.broadcasted_iota(jnp.int32, (PATCH, 4 * PATCH), 1)
    row = lax.broadcasted_iota(jnp.int32, (PATCH, 4 * PATCH), 0)
    spread = jnp.where(lane // 4 == row, 1.0, 0.0).astype(jnp.bfloat16)
    repeated = jnp.dot(letters, spread, preferred_element_type=jnp.float32)
    base = (lax.broadcasted_iota(jnp.int32, (1, 4 * PATCH), 1) % 4).astype(jnp.float32)
    return jnp.where(repeated == base, 1.0, 0.0).astype(jnp.bfloat16)


def fetch(layer, ids, w_hbm, weights, sems):
    width = weights.shape[2]
    copies = []
    for t in range(3):
        for k in range(4):
            copies.append(
                pltpu.make_async_copy(
                    w_hbm.at[layer, t, pl.ds((ids[0] ^ k) * width, width), :],
                    weights.at[t, pl.ds(k * width, width), :],
                    sems.at[t, k],
                )
            )
            copies[-1].start()
    for copy in copies:
        copy.wait()


def prepare(letters, onehot):
    onehot[...] = one_hot(letters[...])


def first_layer(span, bins, count, ids, onehot, halo, own_a, own_b, w1, w2a, w2b, w3a, w3b, gains, weights, out, normed, stream):
    low, high = span
    width = out.shape[1]
    first, last = max(low - HALO, 0), min(high + HALO, bins + 2 * HALO)
    rows = last - first
    clear(normed, 0, PAD)
    clear(normed, PAD + rows, PAD)
    stem = jnp.concatenate(
        [
            jnp.concatenate([own_a[...], own_b[...]], axis=0),
            w1[...],
            jnp.concatenate([w2a[...], w2b[...]], axis=0),
            jnp.concatenate([w3a[...], w3b[...]], axis=0),
        ],
        axis=1,
    )
    beyond = one_hot(halo[...])
    if low == 0:
        beyond = jnp.where(ids[1] > 0, beyond, jnp.zeros_like(beyond))
        lines = jnp.concatenate([beyond, onehot[0 : last - HALO, :]], axis=0)
    else:
        beyond = jnp.where((ids[1] + 1) * bins < count, beyond, jnp.zeros_like(beyond))
        lines = jnp.concatenate([onehot[first - HALO : bins, :], beyond], axis=0)
    stream[...] = jnp.dot(lines, stem, preferred_element_type=jnp.float32).astype(jnp.bfloat16)

    def read(at, n):
        return [stream[at : at + n, k * width : (k + 1) * width] for k in range(4)]

    norm_segment(ids, 0, read, rows, gains, normed, PAD)
    update = convolve(normed, weights, PAD + low - first, high - low, FIRST_DILATION0)
    total = stream[low - first : high - first, 0:width].astype(jnp.float32) + update
    inside = in_sequence(ids, low, high - low, bins, count)
    out[...] = (total * inside).astype(jnp.bfloat16)


def front(layer, dilation, span, bins, count, ids, *refs):
    pieces, (gains, weights, out, normed) = refs[:4], refs[4:]
    low, high = span
    rows = high + HALO
    clear(normed, 0, PAD)

    def read(at, n):
        return [p[at : at + n, :] for p in pieces]

    norm_segment(ids, layer, read, rows, gains, normed, PAD)
    update = convolve(normed, weights, PAD + low, high - low, dilation)
    total = pieces[0][low:high, :].astype(jnp.float32) + update
    if count:
        total = total * in_sequence(ids, low, high - low, bins, count)
    out[...] = total.astype(jnp.bfloat16)


def back(layer, dilation, span, bins, count, ids, *refs):
    fronts, backs, (gains, weights, out, normed) = refs[:4], refs[4:8], refs[8:]
    low, high = span
    first = low - HALO
    joint = fronts[0].shape[0]
    rows = joint + backs[0].shape[0] - first
    clear(normed, PAD + rows, PAD)

    def read_front(at, n):
        return [p[first + at : first + at + n, :] for p in fronts]

    def read_back(at, n):
        return [p[at : at + n, :] for p in backs]

    norm_segment(ids, layer, read_front, joint - first, gains, normed, PAD)
    norm_segment(ids, layer, read_back, backs[0].shape[0], gains, normed, PAD + joint - first)
    update = convolve(normed, weights, PAD + HALO, high - low, dilation)
    own = jnp.concatenate([fronts[0][low:joint, :], backs[0][0 : high - joint, :]], axis=0)
    total = own.astype(jnp.float32) + update
    if count:
        total = total * in_sequence(ids, low, high - low, bins, count)
    out[...] = total.astype(jnp.bfloat16)


def gradient(stream, upstream):
    return lax.dot_general(
        stream, upstream, (((0,), (0,)), ((), ())), preferred_element_type=jnp.float32
    )


def last_front(span, bins, ids, *refs):
    refs, (upstream, out, grad, normed) = refs[:6], refs[6:]
    front(2, 4 * FIRST_DILATION0, span, bins, 0, ids, *refs, out, normed)
    low, high = span
    grad[...] = gradient(out[...], upstream[low - HALO : high - HALO, :])


def last_back(span, bins, ids, *refs):
    refs, (upstream, before, out, g0, g1, g2, g3, normed, grad) = refs[:10], refs[10:]
    back(2, 4 * FIRST_DILATION0, span, bins, 0, ids, *refs, out, normed)
    low, high = span
    grad[...] = before[...] + gradient(out[...], upstream[low - HALO : high - HALO, :])
    quarter = g0.shape[0]
    for k, g in enumerate((g0, g1, g2, g3)):
        g[...] = grad[pl.ds(quarter_at(ids, k, quarter), quarter), :].astype(g.dtype)


def quarter_at(ids, k, quarter):
    return pl.multiple_of((ids[2] ^ (ids[2 + k] if k else 0)) * quarter, 8)


def decode(front_rows, back_rows, weights, out):
    cut = front_rows.shape[0]
    for part, first in ((front_rows, 0), (back_rows, cut)):
        value = jnp.dot(part[...], weights[...], preferred_element_type=jnp.float32)
        out[first : first + part.shape[0], :] = value.astype(jnp.bfloat16)


def assemble(ids, p0, p1, p2, p3, out):
    quarter = p0.shape[0]
    for k, p in enumerate((p0, p1, p2, p3)):
        out[pl.ds(quarter_at(ids, k, quarter), quarter), :] = p[...].astype(jnp.float32)


def tie(value, *done):
    return lax.optimization_barrier((value, *done))[0]


def pairs(size, partner):
    return [(i, partner(i)) for i in range(size)]


def call(name, kernel, outs, in_specs, scratch=(), flops=0, megabytes=46):
    many = isinstance(outs, (list, tuple))
    return pl.pallas_call(
        kernel,
        out_shape=tuple(outs) if many else outs,
        in_specs=in_specs,
        out_specs=(VMEM,) * len(outs) if many else VMEM,
        scratch_shapes=list(scratch),
        compiler_params=pltpu.CompilerParams(vmem_limit_bytes=megabytes * 2**20),
        cost_estimate=pl.CostEstimate(flops=flops // 1000 if name != 'fetch' else flops, bytes_accessed=1024, transcendentals=0),
        name=name,
    )


def body(zs, seq_count, bases, stem, gains, conv_weight, dec_weight, upstream):
    bins, width = upstream.shape[1], upstream.shape[2]
    rows = bins + 2 * HALO
    count = bins * seq_count
    bf16, f32 = jnp.bfloat16, jnp.float32
    seq, chan = lax.axis_index("seq"), lax.axis_index("chan")
    x, z = seq // zs, seq % zs
    x_half, z_half = ((x + 1) // 2) % 2, ((z + 1) // 2) % 2
    core = chan % 2
    ids = jnp.stack([chan, seq, x_half * 2 + z_half, 2 - core, 1 + core, 3 + 0 * core])
    ids = ids.astype(jnp.int32)

    across = functools.partial(lax.ppermute, axis_name="chan", perm=pairs(4, lambda i: i ^ 2))
    other_core = functools.partial(lax.ppermute, axis_name="chan", perm=pairs(4, lambda i: i ^ 1))
    far = functools.partial(
        lax.ppermute, axis_name=("section", "chan"), perm=pairs(8, lambda i: i ^ 6)
    )

    letters = bases.reshape(bins, PATCH)
    up = [(i, i + 1) for i in range(seq_count - 1)]
    down = [(j, i) for i, j in up]
    half = stem.shape[0] // 2
    stem_a, stem_b = lax.optimization_barrier((stem[:half], stem[half:]))
    w2a = across(stem_a)
    w2b = far(stem_b)
    w1 = other_core(stem)
    before = lax.ppermute(letters[bins - HALO :], "seq", up)
    def fetched(layer, *done):
        return call(
            "fetch",
            functools.partial(fetch, layer),
            jax.ShapeDtypeStruct(conv_weight.shape[1:], bf16),
            [SMEM, HBM],
            [pltpu.SemaphoreType.DMA((3, 4))],
            flops=10**9,
        )(tie(ids, *done) if done else ids, conv_weight)

    onehot = call(
        "prepare",
        prepare,
        jax.ShapeDtypeStruct((bins, 4 * PATCH), bf16),
        [VMEM],
        flops=10**9,
    )(letters)
    after = lax.ppermute(letters[:HALO], "seq", down)
    weights = fetched(0)
    w2a = tie(w2a, before, after, onehot, weights)
    w3a = other_core(w2a)
    w3b = other_core(w2b)

    def shape(n):
        return jax.ShapeDtypeStruct((n, width), bf16)

    def work(n):
        return 2 * n * 3 * 4 * width * width

    def normed(n):
        return pltpu.VMEM((n + 2 * PAD, 4 * width), bf16)

    def exchange(own):
        return own, other_core(own), across(own)

    def finish(sent, *done):
        own, beside, remote = sent
        remote = tie(remote, *done)
        return own, beside, remote, other_core(remote)

    cut = bins // 2 + (0) * HALO
    inputs = (stem_a, stem_b, w1, w2a, w2b, w3a, w3b, gains, weights)
    part = call(
        "zero_front",
        functools.partial(first_layer, (0, cut), bins, count),
        shape(cut),
        [SMEM] + [VMEM] * 11,
        [normed(cut + HALO), pltpu.VMEM((cut + HALO, 4 * width), bf16)],
        flops=work(cut),
    )(ids, onehot, before, *inputs)
    sent_front = exchange(part)
    part = call(
        "zero_back",
        functools.partial(first_layer, (cut, rows), bins, count),
        shape(rows - cut),
        [SMEM] + [VMEM] * 11,
        [normed(rows - cut + HALO), pltpu.VMEM((rows - cut + HALO, 4 * width), bf16)],
        flops=work(rows - cut),
    )(ids, onehot, after, *inputs)
    sent_back = exchange(part)
    weights = fetched(1, part)
    fronts = finish(sent_front, part, weights)

    cut = cut - HALO
    layer = (1, 2 * FIRST_DILATION0)
    part = call(
        "one_front",
        functools.partial(front, *layer, (0, cut), bins, count),
        shape(cut),
        [SMEM] + [VMEM] * 6,
        [normed(cut + HALO)],
        flops=work(cut),
    )(ids, *fronts, gains, weights)
    sent_front = exchange(part)
    backs = finish(sent_back, part)
    part = call(
        "one_back",
        functools.partial(back, *layer, (cut, rows), bins, count),
        shape(rows - cut),
        [SMEM] + [VMEM] * 10,
        [normed(rows - cut + HALO)],
        flops=work(rows - cut),
    )(ids, *fronts, *backs, gains, weights)
    sent_back = exchange(part)
    weights = fetched(2, part)
    fronts = finish(sent_front, part, weights)

    cut = cut - HALO
    front_rows, front_grad = call(
        "two_front",
        functools.partial(last_front, (HALO, cut), bins),
        [shape(cut - HALO), jax.ShapeDtypeStruct((width, width), f32)],
        [SMEM] + [VMEM] * 7,
        [normed(cut + HALO)],
        flops=work(cut - HALO),
    )(ids, *fronts, gains, weights, upstream[0])
    backs = finish(sent_back, front_rows)
    back_rows, g0, g1, g2, g3 = call(
        "two_back",
        functools.partial(last_back, (cut, rows - HALO), bins),
        [shape(rows - HALO - cut), jax.ShapeDtypeStruct((width // 4, width), f32)]
        + [shape(width // 4)] * 3,
        [SMEM] + [VMEM] * 12,
        [normed(rows - cut + HALO), pltpu.VMEM((width, width), f32)],
        flops=work(rows - HALO - cut),
    )(ids, *fronts, *backs, gains, weights, upstream[0], front_grad)
    decoded = call(
        "decode",
        decode,
        shape(bins),
        [VMEM] * 3,
        flops=2 * bins * width * width,
        megabytes=8,
    )(front_rows, back_rows, dec_weight)


    def same(i):
        return i

    def flip(i):
        return i ^ 1

    def xs_near(i):
        return 3 - i

    def zs_near(i):
        return (i + 1) % zs if i % 2 else (i - 1) % zs

    def zs_far(i):
        return {0: 3, 3: 0, 1: 6, 6: 1, 2: 5, 5: 2, 4: 7, 7: 4}[i]

    def swap(own, *moves):
        def partner(i):
            pair, lane = divmod(i, 4)
            section, spot = divmod(pair, seq_count)
            fs, fx, fz = moves[lane % len(moves)]
            spot = fx(spot // zs) * zs + fz(spot % zs)
            return (fs(section) * seq_count + spot) * 4 + lane

        perm = pairs(2 * seq_count * 4, partner)
        return lax.ppermute(own, ("section", "seq", "chan"), perm)

    def swap_three(fx, fz, a, b, c):
        both = swap(c, (same, fx, fz))
        along_x, along_z = (same, fx, same), (same, same, fz)
        return swap(a, along_x, along_z), swap(b, along_z, along_x), both

    def add(a, b):
        return (a.astype(f32) + b.astype(f32)).astype(bf16)

    r1, r2, r3 = swap_three(flip, flip, g1, g2, g3)
    total = (g0 + r1.astype(f32)) + (r2.astype(f32) + r3.astype(f32))
    own = total.astype(bf16)
    r1, r2, r3 = swap_three(xs_near, zs_near, own, own, own)
    total = (own.astype(f32) + r1.astype(f32)) + (r2.astype(f32) + r3.astype(f32))
    own = total.astype(bf16)
    sections, far_z = (flip, same, same), (same, same, zs_far)
    own = add(own, swap(own, sections, far_z))
    own = add(own, swap(own, far_z, sections))
    r1, r2, r3 = swap_three(flip, flip, own, own, own)
    weight_grad = call(
        "assemble",
        assemble,
        jax.ShapeDtypeStruct((width, width), f32),
        [SMEM] + [VMEM] * 4,
        megabytes=8,
    )(ids, own, r1, r2, r3)
    return (decoded[None], weight_grad)


def solution(mesh):
    placed = (
        P("section", "seq"),
        P(None, "chan"),
        P(),
        P(None, None, None, "chan"),
        P("chan", None),
        P("section", "seq", "chan"),
    )
    seq_count = mesh.shape["seq"]
    return jax.shard_map(
        functools.partial(body, seq_count // 4, seq_count),
        mesh=mesh,
        in_specs=placed,
        out_specs=(P("section", "seq", "chan"), P("chan", None)),
        check_vma=False,
    )
```

```python
import functools

import jax
import jax.numpy as jnp
from jax import lax
from jax.experimental import pallas as pl
from jax.experimental.pallas import tpu as pltpu
from jax.sharding import PartitionSpec as P

PATCH = 128
FIRST_DILATION0 = 2
EPSILON = 1e-06
HALO = 16
STEP = 32
PAD = 16

VMEM = pl.BlockSpec(memory_space=pltpu.VMEM)
SMEM = pl.BlockSpec(memory_space=pltpu.SMEM)
HBM = pl.BlockSpec(memory_space=pltpu.HBM)


def gelu(x):
    inner = x * (0.7978845608028654 + 0.035677408136300125 * (x * x))
    return (0.5 * x) * (1.0 + jnp.tanh(inner))


def in_sequence(ids, first, rows, bins, count):
    bin_at = lax.broadcasted_iota(jnp.int32, (rows, 1), 0) + (ids[1] * bins - HALO + first)
    return jnp.where((bin_at >= 0) & (bin_at < count), 1.0, 0.0)


def norm_rows(ids, layer, pieces, gains, normed, at):
    rows, width = pieces[0].shape
    wide = [p.astype(jnp.float32) for p in pieces]
    total = wide[0] * wide[0]
    for w in wide[1:]:
        total = total + w * w
    inverse = lax.rsqrt(jnp.sum(total, axis=-1, keepdims=True) * (1.0 / (4 * width)) + EPSILON)
    for k, w in enumerate(wide):
        at_lane = pl.multiple_of((ids[0] ^ k) * width, 128)
        value = gelu(w * inverse * gains[layer : layer + 1, pl.ds(at_lane, width)])
        normed[at : at + rows, k * width : (k + 1) * width] = value.astype(jnp.bfloat16)


def norm_segment(ids, layer, read, count, gains, normed, at):
    for first in range(0, count, STEP):
        rows = min(STEP, count - first)
        norm_rows(ids, layer, read(first, rows), gains, normed, at + first)


def convolve(normed, weights, at, rows, dilation):
    update = None
    for t in range(3):
        first = at + (t - 1) * dilation
        part = jnp.dot(
            normed[first : first + rows, :], weights[t], preferred_element_type=jnp.float32
        )
        update = part if update is None else update + part
    return update


def clear(ref, first, rows):
    ref[first : first + rows, :] = jnp.zeros((rows, ref.shape[1]), ref.dtype)


def one_hot(letters):
    letters = letters.astype(jnp.float32).astype(jnp.bfloat16)
    lane = lax.broadcasted_iota(jnp.int32, (PATCH, 4 * PATCH), 1)
    row = lax.broadcasted_iota(jnp.int32, (PATCH, 4 * PATCH), 0)
    spread = jnp.where(lane // 4 == row, 1.0, 0.0).astype(jnp.bfloat16)
    repeated = jnp.dot(letters, spread, preferred_element_type=jnp.float32)
    base = (lax.broadcasted_iota(jnp.int32, (1, 4 * PATCH), 1) % 4).astype(jnp.float32)
    return jnp.where(repeated == base, 1.0, 0.0).astype(jnp.bfloat16)


def fetch(layer, ids, w_hbm, weights, sems):
    width = weights.shape[2]
    copies = []
    for t in range(3):
        for k in range(4):
            copies.append(
                pltpu.make_async_copy(
                    w_hbm.at[layer, t, pl.ds((ids[0] ^ k) * width, width), :],
                    weights.at[t, pl.ds(k * width, width), :],
                    sems.at[t, k],
                )
            )
            copies[-1].start()
    for copy in copies:
        copy.wait()


def prepare(letters, onehot):
    onehot[...] = one_hot(letters[...])


def first_layer(span, bins, count, ids, onehot, halo, own_a, own_b, w1, w2a, w2b, w3a, w3b, gains, weights, out, normed, stream):
    low, high = span
    width = out.shape[1]
    first, last = max(low - HALO, 0), min(high + HALO, bins + 2 * HALO)
    rows = last - first
    clear(normed, 0, PAD)
    clear(normed, PAD + rows, PAD)
    stem = jnp.concatenate(
        [
            jnp.concatenate([own_a[...], own_b[...]], axis=0),
            w1[...],
            jnp.concatenate([w2a[...], w2b[...]], axis=0),
            jnp.concatenate([w3a[...], w3b[...]], axis=0),
        ],
        axis=1,
    )
    beyond = one_hot(halo[...])
    if low == 0:
        beyond = jnp.where(ids[1] > 0, beyond, jnp.zeros_like(beyond))
        lines = jnp.concatenate([beyond, onehot[0 : last - HALO, :]], axis=0)
    else:
        beyond = jnp.where((ids[1] + 1) * bins < count, beyond, jnp.zeros_like(beyond))
        lines = jnp.concatenate([onehot[first - HALO : bins, :], beyond], axis=0)
    stream[...] = jnp.dot(lines, stem, preferred_element_type=jnp.float32).astype(jnp.bfloat16)

    def read(at, n):
        return [stream[at : at + n, k * width : (k + 1) * width] for k in range(4)]

    norm_segment(ids, 0, read, rows, gains, normed, PAD)
    update = convolve(normed, weights, PAD + low - first, high - low, FIRST_DILATION0)
    total = stream[low - first : high - first, 0:width].astype(jnp.float32) + update
    inside = in_sequence(ids, low, high - low, bins, count)
    out[...] = (total * inside).astype(jnp.bfloat16)


def front(layer, dilation, span, bins, count, ids, *refs):
    pieces, (gains, weights, out, normed) = refs[:4], refs[4:]
    low, high = span
    rows = high + HALO
    clear(normed, 0, PAD)

    def read(at, n):
        return [p[at : at + n, :] for p in pieces]

    norm_segment(ids, layer, read, rows, gains, normed, PAD)
    update = convolve(normed, weights, PAD + low, high - low, dilation)
    total = pieces[0][low:high, :].astype(jnp.float32) + update
    if count:
        total = total * in_sequence(ids, low, high - low, bins, count)
    out[...] = total.astype(jnp.bfloat16)


def back(layer, dilation, span, bins, count, ids, *refs):
    fronts, backs, (gains, weights, out, normed) = refs[:4], refs[4:8], refs[8:]
    low, high = span
    first = low - HALO
    joint = fronts[0].shape[0]
    rows = joint + backs[0].shape[0] - first
    clear(normed, PAD + rows, PAD)

    def read_front(at, n):
        return [p[first + at : first + at + n, :] for p in fronts]

    def read_back(at, n):
        return [p[at : at + n, :] for p in backs]

    norm_segment(ids, layer, read_front, joint - first, gains, normed, PAD)
    norm_segment(ids, layer, read_back, backs[0].shape[0], gains, normed, PAD + joint - first)
    update = convolve(normed, weights, PAD + HALO, high - low, dilation)
    own = jnp.concatenate([fronts[0][low:joint, :], backs[0][0 : high - joint, :]], axis=0)
    total = own.astype(jnp.float32) + update
    if count:
        total = total * in_sequence(ids, low, high - low, bins, count)
    out[...] = total.astype(jnp.bfloat16)


def gradient(stream, upstream):
    return lax.dot_general(
        stream, upstream, (((0,), (0,)), ((), ())), preferred_element_type=jnp.float32
    )


def last_front(span, bins, ids, *refs):
    refs, (upstream, out, grad, normed) = refs[:6], refs[6:]
    front(2, 4 * FIRST_DILATION0, span, bins, 0, ids, *refs, out, normed)
    low, high = span
    grad[...] = gradient(out[...], upstream[low - HALO : high - HALO, :])


def last_back(span, bins, ids, *refs):
    refs, (upstream, before, out, g0, g1, g2, g3, normed, grad) = refs[:10], refs[10:]
    back(2, 4 * FIRST_DILATION0, span, bins, 0, ids, *refs, out, normed)
    low, high = span
    grad[...] = before[...] + gradient(out[...], upstream[low - HALO : high - HALO, :])
    quarter = g0.shape[0]
    for k, g in enumerate((g0, g1, g2, g3)):
        g[...] = grad[pl.ds(quarter_at(ids, k, quarter), quarter), :].astype(g.dtype)


def quarter_at(ids, k, quarter):
    return pl.multiple_of((ids[2] ^ (ids[2 + k] if k else 0)) * quarter, 8)


def decode(front_rows, back_rows, weights, out):
    cut = front_rows.shape[0]
    for part, first in ((front_rows, 0), (back_rows, cut)):
        value = jnp.dot(part[...], weights[...], preferred_element_type=jnp.float32)
        out[first : first + part.shape[0], :] = value.astype(jnp.bfloat16)


def assemble(ids, p0, p1, p2, p3, out):
    quarter = p0.shape[0]
    for k, p in enumerate((p0, p1, p2, p3)):
        out[pl.ds(quarter_at(ids, k, quarter), quarter), :] = p[...].astype(jnp.float32)


def tie(value, *done):
    return lax.optimization_barrier((value, *done))[0]


def pairs(size, partner):
    return [(i, partner(i)) for i in range(size)]


def call(name, kernel, outs, in_specs, scratch=(), flops=0, megabytes=46):
    many = isinstance(outs, (list, tuple))
    return pl.pallas_call(
        kernel,
        out_shape=tuple(outs) if many else outs,
        in_specs=in_specs,
        out_specs=(VMEM,) * len(outs) if many else VMEM,
        scratch_shapes=list(scratch),
        compiler_params=pltpu.CompilerParams(vmem_limit_bytes=megabytes * 2**20),
        cost_estimate=pl.CostEstimate(flops=flops // 1000 if name != 'fetch' else flops, bytes_accessed=1024, transcendentals=0),
        name=name,
    )


def body(zs, seq_count, bases, stem, gains, conv_weight, dec_weight, upstream):
    bins, width = upstream.shape[1], upstream.shape[2]
    rows = bins + 2 * HALO
    count = bins * seq_count
    bf16, f32 = jnp.bfloat16, jnp.float32
    seq, chan = lax.axis_index("seq"), lax.axis_index("chan")
    x, z = seq // zs, seq % zs
    x_half, z_half = ((x + 1) // 2) % 2, ((z + 1) // 2) % 2
    core = chan % 2
    ids = jnp.stack([chan, seq, x_half * 2 + z_half, 2 - core, 1 + core, 3 + 0 * core])
    ids = ids.astype(jnp.int32)

    across = functools.partial(lax.ppermute, axis_name="chan", perm=pairs(4, lambda i: i ^ 2))
    other_core = functools.partial(lax.ppermute, axis_name="chan", perm=pairs(4, lambda i: i ^ 1))
    far = functools.partial(
        lax.ppermute, axis_name=("section", "chan"), perm=pairs(8, lambda i: i ^ 6)
    )

    letters = bases.reshape(bins, PATCH)
    up = [(i, i + 1) for i in range(seq_count - 1)]
    down = [(j, i) for i, j in up]
    half = stem.shape[0] // 2
    stem_a, stem_b = lax.optimization_barrier((stem[:half], stem[half:]))
    w2a = across(stem_a)
    w2b = far(stem_b)
    w1 = other_core(stem)
    before = lax.ppermute(letters[bins - HALO :], "seq", up)
    def fetched(layer, *done):
        return call(
            "fetch",
            functools.partial(fetch, layer),
            jax.ShapeDtypeStruct(conv_weight.shape[1:], bf16),
            [SMEM, HBM],
            [pltpu.SemaphoreType.DMA((3, 4))],
            flops=10**9,
        )(tie(ids, *done) if done else ids, conv_weight)

    onehot = call(
        "prepare",
        prepare,
        jax.ShapeDtypeStruct((bins, 4 * PATCH), bf16),
        [VMEM],
        flops=10**9,
    )(letters)
    after = lax.ppermute(letters[:HALO], "seq", down)
    weights = fetched(0)
    w2a = tie(w2a, before, after, onehot, weights)
    w3a = other_core(w2a)
    w3b = other_core(w2b)

    def shape(n):
        return jax.ShapeDtypeStruct((n, width), bf16)

    def work(n):
        return 2 * n * 3 * 4 * width * width

    def normed(n):
        return pltpu.VMEM((n + 2 * PAD, 4 * width), bf16)

    def exchange(own):
        return own, other_core(own), across(own)

    def finish(sent, *done):
        own, beside, remote = sent
        remote = tie(remote, *done)
        return own, beside, remote, other_core(remote)

    cut = bins // 2 + (0) * HALO
    inputs = (stem_a, stem_b, w1, w2a, w2b, w3a, w3b, gains, weights)
    part = call(
        "zero_front",
        functools.partial(first_layer, (0, cut), bins, count),
        shape(cut),
        [SMEM] + [VMEM] * 11,
        [normed(cut + HALO), pltpu.VMEM((cut + HALO, 4 * width), bf16)],
        flops=work(cut),
    )(ids, onehot, before, *inputs)
    sent_front = exchange(part)
    part = call(
        "zero_back",
        functools.partial(first_layer, (cut, rows), bins, count),
        shape(rows - cut),
        [SMEM] + [VMEM] * 11,
        [normed(rows - cut + HALO), pltpu.VMEM((rows - cut + HALO, 4 * width), bf16)],
        flops=work(rows - cut),
    )(ids, onehot, after, *inputs)
    sent_back = exchange(part)
    weights = fetched(1, part)
    fronts = finish(sent_front, part, weights)

    cut = cut - HALO
    layer = (1, 2 * FIRST_DILATION0)
    part = call(
        "one_front",
        functools.partial(front, *layer, (0, cut), bins, count),
        shape(cut),
        [SMEM] + [VMEM] * 6,
        [normed(cut + HALO)],
        flops=work(cut),
    )(ids, *fronts, gains, weights)
    sent_front = exchange(part)
    backs = finish(sent_back, part)
    part = call(
        "one_back",
        functools.partial(back, *layer, (cut, rows), bins, count),
        shape(rows - cut),
        [SMEM] + [VMEM] * 10,
        [normed(rows - cut + HALO)],
        flops=work(rows - cut),
    )(ids, *fronts, *backs, gains, weights)
    sent_back = exchange(part)
    weights = fetched(2, part)
    fronts = finish(sent_front, part, weights)

    cut = cut - HALO
    front_rows, front_grad = call(
        "two_front",
        functools.partial(last_front, (HALO, cut), bins),
        [shape(cut - HALO), jax.ShapeDtypeStruct((width, width), f32)],
        [SMEM] + [VMEM] * 7,
        [normed(cut + HALO)],
        flops=work(cut - HALO),
    )(ids, *fronts, gains, weights, upstream[0])
    backs = finish(sent_back, front_rows)
    back_rows, g0, g1, g2, g3 = call(
        "two_back",
        functools.partial(last_back, (cut, rows - HALO), bins),
        [shape(rows - HALO - cut), jax.ShapeDtypeStruct((width // 4, width), f32)]
        + [shape(width // 4)] * 3,
        [SMEM] + [VMEM] * 12,
        [normed(rows - cut + HALO), pltpu.VMEM((width, width), f32)],
        flops=work(rows - HALO - cut),
    )(ids, *fronts, *backs, gains, weights, upstream[0], front_grad)
    decoded = call(
        "decode",
        decode,
        shape(bins),
        [VMEM] * 3,
        flops=2 * bins * width * width,
        megabytes=8,
    )(front_rows, back_rows, dec_weight)


    def same(i):
        return i

    def flip(i):
        return i ^ 1

    def xs_near(i):
        return 3 - i

    def zs_near(i):
        return (i + 1) % zs if i % 2 else (i - 1) % zs

    def zs_far(i):
        return {0: 3, 3: 0, 1: 6, 6: 1, 2: 5, 5: 2, 4: 7, 7: 4}[i]

    def swap(own, *moves):
        def partner(i):
            pair, lane = divmod(i, 4)
            section, spot = divmod(pair, seq_count)
            fs, fx, fz = moves[lane % len(moves)]
            spot = fx(spot // zs) * zs + fz(spot % zs)
            return (fs(section) * seq_count + spot) * 4 + lane

        perm = pairs(2 * seq_count * 4, partner)
        return lax.ppermute(own, ("section", "seq", "chan"), perm)

    def swap_three(fx, fz, a, b, c):
        both = swap(c, (same, fx, fz))
        along_x, along_z = (same, fx, same), (same, same, fz)
        return swap(a, along_x, along_z), swap(b, along_z, along_x), both

    def add(a, b):
        return (a.astype(f32) + b.astype(f32)).astype(bf16)

    r1, r2, r3 = swap_three(flip, flip, g1, g2, g3)
    total = (g0 + r1.astype(f32)) + (r2.astype(f32) + r3.astype(f32))
    own = total.astype(bf16)
    r1, r2, r3 = swap_three(xs_near, zs_near, own, own, own)
    total = (own.astype(f32) + r1.astype(f32)) + (r2.astype(f32) + r3.astype(f32))
    own = total.astype(bf16)
    sections, far_z = (flip, same, same), (same, same, zs_far)
    own = add(own, swap(own, far_z, sections))
    own = add(own, swap(own, sections, far_z))
    r1, r2, r3 = swap_three(flip, flip, own, own, own)
    weight_grad = call(
        "assemble",
        assemble,
        jax.ShapeDtypeStruct((width, width), f32),
        [SMEM] + [VMEM] * 4,
        megabytes=8,
    )(ids, own, r1, r2, r3)
    return (decoded[None], weight_grad)


def solution(mesh):
    placed = (
        P("section", "seq"),
        P(None, "chan"),
        P(),
        P(None, None, None, "chan"),
        P("chan", None),
        P("section", "seq", "chan"),
    )
    seq_count = mesh.shape["seq"]
    return jax.shard_map(
        functools.partial(body, seq_count // 4, seq_count),
        mesh=mesh,
        in_specs=placed,
        out_specs=(P("section", "seq", "chan"), P("chan", None)),
        check_vma=False,
    )
```
